32 devices in a mesh: group: 4 (over y, x), rank: 8 (over z, core).
Axes of the slice: x: 2, y: 2, z: 4, core: 2. Of those that a mesh axis runs over, the one named last changes fastest.
Arguments:
- a_blocks: bfloat16 [256, 22, 128, 128], P(('group', 'rank')), may hold values from -0.5 to 0.5
- a_cols: int32 [256, 22], P(('group', 'rank')), may hold values from 0 to 71, as said below
- p_rows: bfloat16 [256, 128, 128], P(('group', 'rank')), may hold values from -1.1953125 to 1.1953125
- p_cols: int32 [256, 4], P(('group', 'rank')), may hold values from 0 to 127, as said below
- send_rows: int32 [32, 32, 2], P(('group', 'rank')), may hold values from -1 to 7, as said below
- c_cols: int32 [128, 27], P('group'), may hold values from 0 to 127, as said below
Outputs:
- coarse: float32 [128, 32, 864], P(('group', 'rank'))
The draws below stay inside these ranges and needn't reach their ends.
Inputs may be any that keep to these rules, and one draw needn't show every extreme that they name: `a_cols`: an entry t of 8 or more names slot t - 8 of what the row's device receives, ordered by sending device then slot; every slot whose send_rows entry is not -1 is named by exactly one entry of the receiving device, and no entry names a slot whose entry is -1. `send_rows`: -1 marks an empty slot; a device sends nothing to itself. `p_cols`: the coarse block columns of fine block rows on group g lie in g * 32 to g * 32 + 31. `c_cols`: the 27 block columns of a coarse block row are distinct.
All inputs are finite; a program needn't handle non-finite values.
Results may differ from the reference program's by a relative error of at most 0.0029.
Values may be sent and summed in bfloat16 or wider, within the bound.
No kernel may reach another device: no remote copies, remote signals or barrier semaphores. Data moves between devices by JAX's collectives and lax.ppermute only.
A program may use at most 128 MiB of HBM per device.

```python
import jax
import jax.numpy as jnp
from jax import lax

FB_DEV = 8
CB_DEV = 4
B = 128
KA = 22
KP = 4
BC = 32
KC = 27
CAP = 2
NF = 256
NC = 128
N_GROUP = 4
N_RANK = 8


def routing(key):
    dev_count = N_GROUP * N_RANK
    entries = FB_DEV * KA
    slot_total = dev_count * CAP
    base_key = jax.random.fold_in(key, 101)
    key_weight = jax.random.fold_in(base_key, 1)
    key_roll = jax.random.fold_in(base_key, 2)
    key_rows = jax.random.fold_in(base_key, 3)
    key_local = jax.random.fold_in(base_key, 4)
    key_order = jax.random.fold_in(base_key, 5)
    shift_by = jax.random.randint(key_weight, (dev_count,), 0, 4)
    weight = jnp.left_shift(jnp.ones((dev_count,), jnp.int32), shift_by)
    roll_value = jax.random.randint(key_roll, (dev_count, dev_count, CAP), 0, 16 * slot_total)
    limit = weight[:, None, None] * min(2 * slot_total, entries)
    same_dev = jnp.arange(dev_count)[:, None] == jnp.arange(dev_count)[None, :]
    is_live = (roll_value < limit) & jnp.logical_not(same_dev)[:, :, None]
    flat_live = is_live.reshape(dev_count, slot_total).astype(jnp.int32)
    before = jnp.cumsum(flat_live, axis=1) - flat_live
    kept = (flat_live == 1) & (before < entries // 2)
    row_pick = jax.random.randint(key_rows, (dev_count, dev_count, CAP), 0, FB_DEV)
    send_by_reader = jnp.where(kept.reshape(dev_count, dev_count, CAP), row_pick, -1)
    send_rows = jnp.transpose(send_by_reader, (1, 0, 2)).astype(jnp.int32)
    live_count = jnp.sum(kept.astype(jnp.int32), axis=1)
    order = jnp.argsort(1 - kept.astype(jnp.int32), axis=1, stable=True).astype(jnp.int32)
    order = jnp.pad(order, ((0, 0), (0, max(0, entries - slot_total))))[:, :entries]
    position = jnp.arange(entries, dtype=jnp.int32)[None, :]
    local_pick = jax.random.randint(key_local, (dev_count, entries), 0, FB_DEV)
    values = jnp.where(position < live_count[:, None], FB_DEV + order, local_pick)
    scores = jax.random.randint(key_order, (dev_count, entries), 0, 2 ** 20) * entries + position
    shuffle = jnp.argsort(scores, axis=1, stable=True)
    values = jnp.take_along_axis(values, shuffle, axis=1)
    a_cols = values.reshape(dev_count * FB_DEV, KA).astype(jnp.int32)
    return (a_cols, send_rows)


def draw_a_cols(key, part):
    a_cols, send_rows = routing(key)
    return a_cols


def draw_send_rows(key, part):
    a_cols, send_rows = routing(key)
    return send_rows


def draw_p_cols(key, part):
    group_span = CB_DEV * N_RANK
    row_total = N_GROUP * N_RANK * FB_DEV
    row_index = jnp.arange(row_total, dtype=jnp.int32)
    device_of = row_index // FB_DEV
    group_of = device_of // N_RANK
    rank_of = device_of % N_RANK
    local_row = row_index % FB_DEV
    slot_number = local_row[:, None] * KP + jnp.arange(KP, dtype=jnp.int32)[None, :]
    kind = slot_number % 4
    random_rank = jax.random.randint(jax.random.fold_in(key, 7), (row_total, KP), 0, N_RANK)
    within = jax.random.randint(jax.random.fold_in(key, 8), (row_total, KP), 0, CB_DEV)
    rank_grid = jnp.broadcast_to(rank_of[:, None], (row_total, KP))
    target = jnp.where(kind == 0, rank_grid, jnp.where(kind == 1, rank_grid + N_RANK - 1, jnp.where(kind == 2, rank_grid + N_RANK // 2, random_rank))) % N_RANK
    inside = target * CB_DEV + within
    return (group_of[:, None] * group_span + inside).astype(jnp.int32)


def draw_c_cols(key, part):
    dev_count = N_GROUP * N_RANK
    row_total = CB_DEV * N_RANK * N_GROUP
    fine_total = dev_count * FB_DEV
    a_cols, send_rows = routing(key)
    p_cols = draw_p_cols(key, part)
    owners = (jnp.arange(fine_total, dtype=jnp.int32) // FB_DEV)[:, None]
    owner_grid = jnp.broadcast_to(owners, a_cols.shape).astype(jnp.int32)
    is_local = a_cols < FB_DEV
    offset = jnp.maximum(a_cols - FB_DEV, 0).astype(jnp.int32)
    sender = offset // CAP
    slot_index = offset % CAP
    remote = send_rows[sender, owner_grid, slot_index]
    jrow = jnp.where(is_local, owner_grid * FB_DEV + a_cols, sender * FB_DEV + jnp.maximum(remote, 0)).astype(jnp.int32)
    far_cols = p_cols[jrow]
    near = jnp.broadcast_to(p_cols[:, None, :, None], (fine_total, KA, KP, KP))
    far = jnp.broadcast_to(far_cols[:, :, None, :], (fine_total, KA, KP, KP))
    entry_weight = jnp.where(is_local, 1, 64).astype(jnp.int32)
    weight_grid = jnp.broadcast_to(entry_weight[:, :, None, None], (fine_total, KA, KP, KP)).reshape(-1)
    flat = (near * row_total + far).reshape(-1)
    counts = jnp.zeros((row_total * row_total,), jnp.int32).at[flat].add(weight_grid).reshape(row_total, row_total)
    keys = jax.random.split(jax.random.fold_in(key, 13), row_total)
    breaker = jax.vmap(lambda one_key: jax.random.permutation(one_key, row_total))(keys).astype(jnp.int32)
    scores = counts * row_total + breaker
    top_scores, picked = lax.top_k(scores, KC)
    return picked.astype(jnp.int32)


def block_scale(own_key, extent, cuts, smallest, high):
    loudness, own = 1.0, jax.random.fold_in(own_key, 6)
    for axis_at, parts in cuts:
        steps = jnp.exp(jax.random.uniform(jax.random.fold_in(own, axis_at), (parts,), jnp.float32, smallest / len(cuts), high / len(cuts)))
        loudness = loudness * jnp.repeat(steps, extent[axis_at] // parts).reshape([-1 if axis == axis_at else 1 for axis in range(len(extent))])
    return loudness


def normal_values(rng, dims, width, reach, cuts=(), kind=jnp.bfloat16):
    gain = block_scale(rng, dims, cuts, -0.22, 0.18) if cuts else 1.0
    values = jax.random.normal(rng, dims, jnp.float32) * width * gain
    return jnp.minimum(jnp.maximum(values, -reach), reach).astype(kind)


def setup_inputs(seed: int = 0) -> dict:
    arg_keys = jax.random.split(jax.random.key(seed), 7)
    return {
        "a_blocks": normal_values(arg_keys[0], (NF, KA, B, B), B ** -0.5, 0.5, ((0, 32),)),
        "a_cols": draw_a_cols(jax.random.fold_in(arg_keys[6], 71), 0),
        "p_rows": normal_values(arg_keys[2], (NF, B, KP * BC), 0.2, 1.1953125, ((0, 32),)),
        "p_cols": draw_p_cols(jax.random.fold_in(arg_keys[6], 71), 0),
        "send_rows": draw_send_rows(jax.random.fold_in(arg_keys[6], 71), 0),
        "c_cols": draw_c_cols(jax.random.fold_in(arg_keys[6], 71), 0),
    }


def source_rows(a_cols, send_rows):
    owners = (jnp.arange(NF, dtype=jnp.int32) // FB_DEV)[:, None]
    owner_grid = jnp.broadcast_to(owners, a_cols.shape).astype(jnp.int32)
    is_local = a_cols < FB_DEV
    offset = jnp.maximum(a_cols - FB_DEV, 0).astype(jnp.int32)
    sender = (offset // CAP).astype(jnp.int32)
    slot_index = (offset % CAP).astype(jnp.int32)
    remote = send_rows[sender, owner_grid, slot_index]
    return jnp.where(is_local, owner_grid * FB_DEV + a_cols, sender * FB_DEV + remote).astype(jnp.int32)


def reference(a_blocks, a_cols, p_rows, p_cols, send_rows, c_cols):
    devices = N_GROUP * N_RANK
    source = source_rows(a_cols, send_rows)

    def one_device(summed, pieces):
        a_part, src_part, p_part, pc_part = pieces
        weighted = jnp.einsum('ixr,ikxy->ikry', p_part.astype(jnp.float32), a_part.astype(jnp.float32)).astype(jnp.bfloat16)
        fetched = p_rows[src_part].astype(jnp.float32)
        product = jnp.einsum('ikry,ikyc->ikrc', weighted.astype(jnp.float32), fetched)
        product = product.reshape(FB_DEV, KA, KP, BC, KP, BC)
        far_cols = p_cols[src_part]
        targets = c_cols[pc_part]
        select = (targets[:, :, :, None, None] == far_cols[:, None, None, :, :]).astype(jnp.float32)
        merged = jnp.einsum('imskn,ikmanb->imasb', select, product, precision=lax.Precision.HIGHEST)
        merged = merged.reshape(FB_DEV * KP, BC, KC * BC)
        return summed.at[pc_part.reshape(-1)].add(merged), None

    pieces = (a_blocks.reshape(devices, FB_DEV, KA, B, B),
              source.reshape(devices, FB_DEV, KA),
              p_rows.reshape(devices, FB_DEV, B, KP * BC),
              p_cols.reshape(devices, FB_DEV, KP))
    summed, _ = lax.scan(one_device, jnp.zeros((NC, BC, KC * BC), jnp.float32), pieces)
    return summed
```

```python
import functools

import jax
import jax.numpy as jnp
from jax import lax
from jax.experimental import pallas as pl
from jax.experimental.pallas import tpu as pltpu
from jax.sharding import Mesh, PartitionSpec as P

NT = (((1,), (1,)), ((), ()))
NN = (((1,), (0,)), ((), ()))


def prep_kernel(wanted_ref, pcols_ref, p_ref, pt_ref, out_ref, cols_ref):
    rows, span, width = p_ref.shape
    slots, parts = wanted_ref.shape[0], pcols_ref.shape[1]
    row_id = lax.broadcasted_iota(jnp.int32, (width, width), 0)
    col_id = lax.broadcasted_iota(jnp.int32, (width, width), 1)
    unit = jnp.where(row_id == col_id, 1.0, 0.0).astype(p_ref.dtype)
    for row in range(rows):
        flipped = lax.dot_general(unit, p_ref[row], NT, preferred_element_type=jnp.float32)
        pt_ref[row] = flipped.astype(pt_ref.dtype)

    def fill(slot, carry):
        row = jnp.maximum(wanted_ref[slot], 0)
        out_ref[slot] = pt_ref[row]
        for part in range(parts):
            cols_ref[slot * parts + part] = pcols_ref[row, part]
        return carry

    lax.fori_loop(0, slots, fill, 0)


def prepare(p_rows, p_cols, wanted):
    rows, span, width = p_rows.shape
    slots, parts = wanted.shape[0], p_cols.shape[1]
    vmem, smem = pl.BlockSpec(memory_space=pltpu.VMEM), pl.BlockSpec(memory_space=pltpu.SMEM)
    return pl.pallas_call(
        prep_kernel,
        out_shape=(
            jax.ShapeDtypeStruct((rows, width, span), p_rows.dtype),
            jax.ShapeDtypeStruct((slots, width, span), p_rows.dtype),
            jax.ShapeDtypeStruct((slots * parts,), jnp.int32),
        ),
        in_specs=[smem, smem, vmem],
        out_specs=(vmem, vmem, smem),
        compiler_params=pltpu.CompilerParams(vmem_limit_bytes=48 << 20),
        name="prep",
    )(wanted, p_cols, p_rows)


def weigh_kernel(pt_ref, a_ref, w_ref):
    left = pt_ref[0]
    for k in range(a_ref.shape[1]):
        w_ref[0, k] = lax.dot_general(
            left, a_ref[0, k], NN, preferred_element_type=jnp.float32
        ).astype(w_ref.dtype)


def weigh(pt, a_blocks):
    rows, cols, span, _ = a_blocks.shape
    width = pt.shape[1]
    return pl.pallas_call(
        weigh_kernel,
        grid=(rows,),
        out_shape=jax.ShapeDtypeStruct((rows, cols, width, span), jnp.bfloat16),
        in_specs=[
            pl.BlockSpec((1, width, span), lambda i: (i, 0, 0)),
            pl.BlockSpec((1, cols, span, span), lambda i: (i, 0, 0, 0)),
        ],
        out_specs=pl.BlockSpec((1, cols, width, span), lambda i: (i, 0, 0, 0)),
        cost_estimate=pl.CostEstimate(
            flops=2 * rows * cols * span * span * width,
            bytes_accessed=2 * a_blocks.size * 2,
            transcendentals=0,
        ),
        name="weigh",
    )(pt, a_blocks)


def merge_kernel(
    place_ref, acols_ref, pcols_ref, far_ref, ccols_ref, w_ref, local_ref, arrived_ref,
    keep_ref, send_ref, table, dense, panel, rounded, sems,
):
    step, steps = pl.program_id(0), pl.num_programs(0)
    fine_rows, part_count = pcols_ref.shape
    block_cols, width = w_ref.shape[1], w_ref.shape[2]
    span = width // part_count
    pattern = ccols_ref.shape[1]
    chips = keep_ref.shape[0]
    own_rows = width // span
    core, base = place_ref[0], place_ref[1]

    @pl.when(step == 0)
    def _():
        near = pltpu.make_async_copy(local_ref, table.at[pl.ds(0, fine_rows)], sems.at[0])
        far = pltpu.make_async_copy(
            arrived_ref, table.at[pl.ds(fine_rows, arrived_ref.shape[0])], sems.at[1]
        )
        near.start()
        far.start()
        panel[...] = jnp.zeros_like(panel)
        near.wait()
        far.wait()

    dense[...] = jnp.zeros_like(dense)
    for k in range(block_cols):
        source = acols_ref[step, k]
        product = lax.dot_general(
            table[source], w_ref[0, k], NT, preferred_element_type=jnp.float32
        )
        for n in range(part_count):
            at = pl.ds(pl.multiple_of(far_ref[source * part_count + n] * span, span), span)
            dense[at, :] += product[n * span : (n + 1) * span, :]

    lane_group = lax.broadcasted_iota(jnp.int32, (span, width), 1) // span
    for m in range(part_count):
        row = pcols_ref[step, m] - base
        owner, within = row // own_rows, lax.rem(row, own_rows)
        shift = lax.rem(within + part_count - m, part_count) * span
        here = lane_group == within
        for s in range(pattern):
            at = pl.ds(pl.multiple_of(ccols_ref[row, s] * span, span), span)
            moved = pltpu.roll(dense[at, :], shift, 1)
            panel[owner, s * span : (s + 1) * span, :] += jnp.where(here, moved, 0.0)

    @pl.when(step == steps - 1)
    def _():
        copies = []
        for chip in range(chips):
            copies.append(
                pltpu.make_async_copy(
                    panel.at[2 * chip + core], keep_ref.at[chip], sems.at[2 + chip]
                )
            )
            copies[-1].start()
        for chip in range(chips):
            rounded[chip] = panel[2 * chip + 1 - core].astype(rounded.dtype)
        out = pltpu.make_async_copy(rounded, send_ref, sems.at[0])
        out.start()
        for copy in copies:
            copy.wait()
        out.wait()


def merge(place, a_cols, p_cols, far_cols, c_cols, weighted, local, arrived, chips, all_cols):
    rows, cols, width, span = weighted.shape
    parts = p_cols.shape[1]
    small = width // parts
    pattern = c_cols.shape[1]
    slots = arrived.shape[0]
    hbm = pl.BlockSpec(memory_space=pl.ANY)
    return pl.pallas_call(
        merge_kernel,
        out_shape=(
            jax.ShapeDtypeStruct((chips, pattern * small, width), jnp.float32),
            jax.ShapeDtypeStruct((chips, pattern * small, width), jnp.bfloat16),
        ),
        grid_spec=pltpu.PrefetchScalarGridSpec(
            num_scalar_prefetch=5,
            grid=(rows,),
            in_specs=[
                pl.BlockSpec((1, cols, width, span), lambda i, *_: (i, 0, 0, 0)),
                hbm,
                hbm,
            ],
            out_specs=(hbm, hbm),
            scratch_shapes=[
                pltpu.VMEM((rows + slots, width, span), local.dtype),
                pltpu.VMEM((all_cols * small, width), jnp.float32),
                pltpu.VMEM((2 * chips, pattern * small, width), jnp.float32),
                pltpu.VMEM((chips, pattern * small, width), jnp.bfloat16),
                pltpu.SemaphoreType.DMA((2 + chips,)),
            ],
        ),
        compiler_params=pltpu.CompilerParams(vmem_limit_bytes=56 << 20),
        name="merge",
    )(place, a_cols, p_cols, far_cols, c_cols, weighted, local, arrived)


def pair_kernel(place_ref, keep_ref, got_ref, mine_ref, *out_refs):
    chips = keep_ref.shape[0]
    chip = place_ref[2]
    mine_ref[...] = keep_ref[chip] + got_ref[chip].astype(jnp.float32)
    for off, out_ref in enumerate(out_refs):
        at = jnp.bitwise_xor(chip, off + 1)
        out_ref[...] = (keep_ref[at] + got_ref[at].astype(jnp.float32)).astype(out_ref.dtype)


def pair(place, keep, got):
    chips, tall, width = keep.shape
    vmem, smem = pl.BlockSpec(memory_space=pltpu.VMEM), pl.BlockSpec(memory_space=pltpu.SMEM)
    return pl.pallas_call(
        pair_kernel,
        out_shape=(jax.ShapeDtypeStruct((tall, width), jnp.float32),)
        + (jax.ShapeDtypeStruct((tall, width), jnp.bfloat16),) * (chips - 1),
        in_specs=[smem, vmem, vmem],
        out_specs=(vmem,) * chips,
        compiler_params=pltpu.CompilerParams(vmem_limit_bytes=56 << 20),
        name="pair",
    )(place, keep, got)


def last_kernel(mine_ref, *refs):
    terms, out_ref = refs[:-1], refs[-1]
    total = mine_ref[...]
    for term in terms:
        total = total + term[...].astype(jnp.float32)
    out_ref[...] = total.T.reshape(out_ref.shape)


def last(mine, terms, own_rows):
    tall, width = mine.shape
    vmem = pl.BlockSpec(memory_space=pltpu.VMEM)
    return pl.pallas_call(
        last_kernel,
        out_shape=jax.ShapeDtypeStruct((own_rows, width // own_rows, tall), jnp.float32),
        in_specs=[vmem] * (1 + len(terms)),
        out_specs=vmem,
        compiler_params=pltpu.CompilerParams(vmem_limit_bytes=56 << 20),
        name="last",
    )(mine, *terms)


def local(chips, groups, a_blocks, a_cols, p_rows, p_cols, send_rows, c_cols):
    parts, width = p_cols.shape[1], p_rows.shape[2]
    group_rows = c_cols.shape[0]
    everyone = ("group", "chip", "core")
    chip = lax.axis_index("chip")
    place = jnp.stack(
        [lax.axis_index("core"), lax.axis_index("group") * group_rows, chip]
    ).astype(jnp.int32)
    pt, outgoing, out_cols = prepare(p_rows, p_cols, send_rows.reshape(-1))
    arrived = lax.all_to_all(outgoing, everyone, split_axis=0, concat_axis=0, tiled=True)
    arrived_cols = lax.all_to_all(out_cols.reshape(-1, 2 * parts), everyone, split_axis=0, concat_axis=0, tiled=True)
    far_cols = jnp.concatenate([p_cols.reshape(-1), arrived_cols.reshape(-1)])
    weighted = weigh(pt, a_blocks)
    keep, give = merge(
        place, a_cols, p_cols, far_cols, c_cols, weighted, pt, arrived, chips, group_rows * groups
    )
    got = lax.ppermute(give, "core", [(0, 1), (1, 0)])
    own_rows = group_rows // (2 * chips)
    if chips == 4:
        mine, *out = pair(place, keep, got)
        terms = [
            lax.ppermute(piece, "chip", [(q, q ^ (off + 1)) for q in range(chips)])
            for off, piece in enumerate(out)
        ]
        return last(mine, terms, own_rows)
    both = keep + got.astype(jnp.float32)
    mine = lax.dynamic_index_in_dim(both, chip, 0, keepdims=False)
    came = lax.all_to_all(
        both.astype(jnp.bfloat16), "chip", split_axis=0, concat_axis=0, tiled=True
    ).astype(jnp.float32)
    other = jnp.arange(chips)[:, None, None] != chip
    return last(mine + jnp.sum(jnp.where(other, came, 0.0), 0), [], own_rows)


def solution(mesh):
    groups, ranks = mesh.shape["group"], mesh.shape["rank"]
    chips = ranks // 2
    fine = Mesh(mesh.devices.reshape(groups, chips, 2), ("group", "chip", "core"))
    every = ("group", "chip", "core")
    in_specs = (P(every), P(every), P(every), P(every), P(every), P("group"))
    return jax.shard_map(
        functools.partial(local, chips, groups),
        mesh=fine,
        in_specs=in_specs,
        out_specs=P(every),
        check_vma=False,
    )
```

```python
import functools
import math

import jax
import jax.numpy as jnp
from jax import lax
from jax.experimental import pallas as pl
from jax.experimental.pallas import tpu as pltpu
from jax.sharding import Mesh, PartitionSpec as P

NT = (((1,), (1,)), ((), ()))
NN = (((1,), (0,)), ((), ()))


VMEM_SLACK = 4 << 20
VMEM_MOST = 56 << 20
FAR_MOST = 54 << 20


def whole(*shape):
    return pl.BlockSpec(shape, lambda *_: (0,) * len(shape))


def room(*arrays):
    return VMEM_SLACK + sum(math.prod(shape) * jnp.dtype(kind).itemsize for shape, kind in arrays)


def flip(rows_ref, unit, row):
    return lax.dot_general(
        unit, rows_ref[row], NT, preferred_element_type=jnp.float32
    ).astype(rows_ref.dtype)


def identity(width, kind):
    row_id = lax.broadcasted_iota(jnp.int32, (width, width), 0)
    col_id = lax.broadcasted_iota(jnp.int32, (width, width), 1)
    return jnp.where(row_id == col_id, 1.0, 0.0).astype(kind)


def device_of(place_ref, hop, half):
    group = jnp.bitwise_xor(place_ref[5], hop >> 1)
    low = jnp.bitwise_xor(place_ref[6], hop & 1)
    return group, ((group * 2 + half) * 2 + low) * 2


def pack_two_kernel(peers, slots, parts, place_ref, own_ref, other_ref, p_ref, q_ref, *refs):
    outs, pt_ref, table = refs[:8], refs[8], refs[9]
    rows, span, width = p_ref.shape
    core, base, half = place_ref[0], place_ref[1], place_ref[3]
    unit = identity(width, p_ref.dtype)
    for row in range(rows):
        mine = flip(p_ref, unit, row)
        table[core * rows + row] = mine
        table[(1 - core) * rows + row] = flip(q_ref, unit, row)
        pt_ref[row] = mine
    tail = outs[0].shape[1] - slots * width
    lane = lax.broadcasted_iota(jnp.int32, (tail, span), 1)
    for hop, out_ref in enumerate(outs):
        _, device = device_of(place_ref, hop, half)
        for source in range(2):
            note = jnp.zeros((tail, span), jnp.int32)
            mine = core == source
            for slot in range(slots):
                at = slot * peers + device + core
                row = jnp.maximum(jnp.where(mine, own_ref[at], other_ref[at]), 0)
                out_ref[source, slot * width : (slot + 1) * width, :] = table[source * rows + row]
                for part in range(parts):
                    spot = slots * peers + part * rows + row
                    column = jnp.where(mine, own_ref[spot], other_ref[spot]) - base
                    note = jnp.where(lane == slot * parts + part, column, note)
            out_ref[source, slots * width :, :] = note.astype(jnp.float32).astype(out_ref.dtype)


def pack_two(place, own, other, p_rows, q_rows, peers, slots, parts):
    rows, span, width = p_rows.shape
    vmem, smem = pl.BlockSpec(memory_space=pltpu.VMEM), pl.BlockSpec(memory_space=pltpu.SMEM)
    kind = p_rows.dtype
    piece = (2, slots * width + 16, span)
    outs = [jax.ShapeDtypeStruct(piece, kind)] * 8
    outs.append(jax.ShapeDtypeStruct((rows, width, span), kind))
    return pl.pallas_call(
        functools.partial(pack_two_kernel, peers, slots, parts),
        out_shape=tuple(outs),
        in_specs=[smem, smem, smem, vmem, vmem],
        out_specs=(vmem,) * len(outs),
        scratch_shapes=[pltpu.VMEM((2 * rows, width, span), kind)],
        compiler_params=pltpu.CompilerParams(
            vmem_limit_bytes=room((piece, kind), *[(piece, kind)] * 7, *[(p_rows.shape, kind)] * 6)
        ),
        name="pack_two",
    )(place, own, other, p_rows, q_rows)


def pack_kernel(slots, parts, place_ref, facts_ref, p_ref, out_ref, pt_ref):
    rows, span, width = p_ref.shape
    base, half, low = place_ref[1], place_ref[3], place_ref[4]
    unit = identity(width, p_ref.dtype)
    for row in range(rows):
        pt_ref[row] = flip(p_ref, unit, row)
    tail = out_ref.shape[1] - slots * width
    lane = lax.broadcasted_iota(jnp.int32, (tail, span), 1)
    peers = (facts_ref.shape[0] - parts * rows) // slots

    def fill(index, carry):
        device = (2 * (index // low) + half) * low + lax.rem(index, low)
        note = jnp.zeros((tail, span), jnp.int32)
        for slot in range(slots):
            row = jnp.maximum(facts_ref[slot * peers + device], 0)
            out_ref[index, slot * width : (slot + 1) * width, :] = pt_ref[row]
            for part in range(parts):
                column = facts_ref[slots * peers + part * rows + row] - base
                note = jnp.where(lane == slot * parts + part, column, note)
        out_ref[index, slots * width :, :] = note.astype(jnp.float32).astype(out_ref.dtype)
        return carry

    lax.fori_loop(0, out_ref.shape[0], fill, 0)


def pack(place, facts, p_rows, slots, parts):
    rows, span, width = p_rows.shape
    vmem, smem = pl.BlockSpec(memory_space=pltpu.VMEM), pl.BlockSpec(memory_space=pltpu.SMEM)
    kind = p_rows.dtype
    peers = (facts.shape[0] - parts * rows) // slots
    outgoing = (peers // 2, slots * width + 16, span)
    flipped = (rows, width, span)
    return pl.pallas_call(
        functools.partial(pack_kernel, slots, parts),
        out_shape=(jax.ShapeDtypeStruct(outgoing, kind), jax.ShapeDtypeStruct(flipped, kind)),
        in_specs=[smem, smem, vmem],
        out_specs=(vmem, vmem),
        compiler_params=pltpu.CompilerParams(
            vmem_limit_bytes=room((outgoing, kind), *[(flipped, kind)] * 3)
        ),
        name="pack",
    )(place, facts, p_rows)


def distinct(columns, blocks, dump):
    columns, blocks = list(columns), list(blocks)
    for n in range(1, len(columns)):
        again = jnp.bool_(False)
        for before in range(n):
            same = columns[n] == columns[before]
            blocks[before] = blocks[before] + jnp.where(same, blocks[n], 0.0)
            again = again | same
        columns[n] = jnp.where(again, dump, columns[n])
    return columns, blocks


def near_kernel(
    first_row, resumed, place_ref, acols_ref, pcols_ref, ccols_ref, *refs
):
    if resumed:
        where_in, pt_ref, a_ref, panel_in, far_in, panel_out, far_out, where_ref = refs[:8]
        dense, panel, far, weights, products, sems = refs[8:]
        slot_of_ref = ctable_ref = None
    else:
        ctable_ref, pt_ref, a_ref, panel_out, far_out, where_ref, slot_of_ref = refs[:7]
        dense, panel, far, weights, products, sems = refs[7:]
    step, steps = pl.program_id(0), pl.num_programs(0)
    fine_row = step + first_row
    parts, fine_rows = pcols_ref.shape
    block_cols, width = a_ref.shape[1], pt_ref.shape[1]
    span = width // parts
    pattern = ccols_ref.shape[1]
    slots = far_out.shape[0]
    own_rows = width // span
    base = place_ref[1]
    dump = dense.shape[0] // span - 1
    if resumed:
        load_panel = pltpu.make_async_copy(panel_in, panel, sems.at[0])
        load_far = pltpu.make_async_copy(far_in, far.at[pl.ds(0, slots)], sems.at[1])

    @pl.when(step == 0)
    def _():
        if resumed:
            load_panel.start()
            load_far.start()
        else:
            panel[...] = jnp.zeros_like(panel)
            far[...] = jnp.zeros_like(far)
            column = lax.broadcasted_iota(jnp.int32, slot_of_ref.shape, 1)
            found = jnp.full(slot_of_ref.shape, pattern, jnp.int32)
            for s in range(pattern):
                found = jnp.where(column == ctable_ref[:, s : s + 1], s, found)
            slot_of_ref[...] = found

        def begin(slot, carry):
            where_ref[slot] = where_in[slot] if resumed else fine_rows
            return carry

        lax.fori_loop(0, slots, begin, 0)

    dense[...] = jnp.zeros_like(dense)
    left = pt_ref[fine_row]
    for k in range(0, block_cols, 2):
        ahead = range(k, min(k + 2, block_cols))
        weighted = lax.dot_general(
            left,
            jnp.concatenate([a_ref[0, j] for j in ahead], axis=1),
            NN,
            preferred_element_type=jnp.float32,
        ).astype(far.dtype)
        for j in ahead:
            weights[j] = weighted[:, (j - k) * width : (j - k + 1) * width]
    for k in range(block_cols):
        source = acols_ref[fine_row, k]
        row = jnp.where(source >= fine_rows, 0, source)
        products[k] = lax.dot_general(
            pt_ref[row], weights[k], NT, preferred_element_type=jnp.float32
        )
    if resumed:

        @pl.when(step == 0)
        def _():
            load_panel.wait()
            load_far.wait()

    for k in range(block_cols):
        source = acols_ref[fine_row, k]
        is_far = source >= fine_rows
        slot = jnp.where(is_far, source - fine_rows, slots)
        far[slot] = weights[k]
        where_ref[slot] = fine_row
        row = jnp.where(is_far, 0, source)
        columns, blocks = distinct(
            [pcols_ref[n, row] for n in range(parts)],
            [products[k, n * span : (n + 1) * span, :] for n in range(parts)],
            dump,
        )
        places = [
            pl.ds(pl.multiple_of(jnp.where(is_far, dump, column) * span, span), span)
            for column in columns
        ]
        sums = [dense[at, :] + block for at, block in zip(places, blocks)]
        for at, value in zip(places, sums):
            dense[at, :] = value

    lane_group = lax.broadcasted_iota(jnp.int32, (span, width), 1) // span
    for m in range(parts):
        row = pcols_ref[m, fine_row] - base
        owner, within = row // own_rows, lax.rem(row, own_rows)
        shift = lax.rem(within + parts - m, parts) * span
        here = lane_group == within
        for first in range(0, pattern, 9):
            chunk = range(first, min(first + 9, pattern))
            sums = []
            for s in chunk:
                at = pl.ds(pl.multiple_of(ccols_ref[row, s] * span, span), span)
                moved = pltpu.roll(dense[at, :], shift, 1)
                sums.append(
                    panel[owner, s * span : (s + 1) * span, :] + jnp.where(here, moved, 0.0)
                )
            for s, value in zip(chunk, sums):
                panel[owner, s * span : (s + 1) * span, :] = value

    @pl.when(step == steps - 1)
    def _():
        one = pltpu.make_async_copy(panel, panel_out, sems.at[0])
        two = pltpu.make_async_copy(far.at[pl.ds(0, slots)], far_out, sems.at[1])
        one.start()
        two.start()
        one.wait()
        two.wait()


def near(first_row, rows_here, place, a_cols, pcols_t, c_cols, pt, a_blocks, owners, all_cols, slots, before):
    rows, cols, span, _ = a_blocks.shape
    parts, width = pcols_t.shape[0], pt.shape[1]
    small = width // parts
    group_rows, pattern = c_cols.shape
    tall = (pattern + 1) * small
    hbm, smem = pl.BlockSpec(memory_space=pltpu.HBM), pl.BlockSpec(memory_space=pltpu.SMEM)
    out_shape = [
        jax.ShapeDtypeStruct((owners, tall, width), jnp.float32),
        jax.ShapeDtypeStruct((slots, width, span), jnp.bfloat16),
        jax.ShapeDtypeStruct((slots + 1,), jnp.int32),
    ]
    out_specs = [hbm, hbm, smem]
    in_specs = [
        whole(rows, width, span),
        pl.BlockSpec((1, cols, span, span), lambda i, *_: (i + first_row, 0, 0, 0)),
    ]
    scalars = [place, a_cols, pcols_t, c_cols]
    if before is None:
        in_specs.insert(0, whole(group_rows, pattern))
        operands = [c_cols, pt, a_blocks]
        out_shape.append(jax.ShapeDtypeStruct((group_rows, all_cols + 128), jnp.int32))
        out_specs.append(whole(group_rows, all_cols + 128))
    else:
        scalars.append(before[2])
        operands = [pt, a_blocks, before[0], before[1]]
        in_specs += [hbm, hbm]
    scratch = [
        (((all_cols + 1) * small, width), jnp.float32),
        ((owners, tall, width), jnp.float32),
        ((slots + 1, width, span), jnp.bfloat16),
        ((cols, width, span), jnp.bfloat16),
        ((cols, width, width), jnp.float32),
    ]
    return pl.pallas_call(
        functools.partial(near_kernel, first_row, before is not None),
        out_shape=tuple(out_shape),
        grid_spec=pltpu.PrefetchScalarGridSpec(
            num_scalar_prefetch=len(scalars),
            grid=(rows_here,),
            in_specs=in_specs,
            out_specs=tuple(out_specs),
            scratch_shapes=[pltpu.VMEM(*one) for one in scratch] + [pltpu.SemaphoreType.DMA((2,))],
        ),
        compiler_params=pltpu.CompilerParams(
            vmem_limit_bytes=VMEM_MOST
        ),
        cost_estimate=pl.CostEstimate(flops=1, bytes_accessed=1, transcendentals=0),
        name="near",
    )(*scalars, *operands)


def far_kernel(
    counts, steps, place_ref, where_ref, pcols_ref, slot_of_ref, far_in, panel_in, *refs
):
    arrived = refs[: len(counts)]
    keep_ref, send_ref, panel, far_ref, products, columns, columns_s, sems, *extra = refs[
        len(counts) :
    ]
    hidden = bool(extra)
    gathered = extra[0] if hidden else panel
    step = 0 if steps == 1 else pl.program_id(0)
    parts, fine_rows = pcols_ref.shape
    width = far_ref.shape[1]
    small = width // parts
    chips, tall = keep_ref.shape[0], keep_ref.shape[1]
    pattern = tall // small
    own_rows = width // small
    core, base, half, low = (place_ref[at] for at in (0, 1, 3, 4))
    total = sum(counts)
    slots = products.shape[0] // total
    unlisted = slot_of_ref.shape[1] - 1
    load = pltpu.make_async_copy(panel_in, panel, sems.at[0])
    load_far = pltpu.make_async_copy(far_in, far_ref, sems.at[1])

    def spread(peer, which):
        group = peer // low
        return group, (2 * group + which) * low + lax.rem(peer, low)

    def source_of(index):
        if len(counts) == 2:
            each = counts[0]
            peer = step * each + lax.rem(index, each)
            return spread(peer, jnp.bitwise_xor(half, index // each))
        near_by = 2 * (len(counts) - 1)
        hop = jnp.minimum(index, near_by - 1) // 2
        group_a, device_a = device_of(place_ref, hop, half)
        group_b, device_b = spread(jnp.maximum(index - near_by, 0), 1 - half)
        first = index < near_by
        return (
            jnp.where(first, group_a, group_b),
            jnp.where(first, device_a + lax.rem(index, 2), device_b),
        )

    def at_start(action):
        action() if steps == 1 else pl.when(step == 0)(action)

    def begin():
        load_far.start()
        load.start()

    at_start(begin)
    order = [(a, e) for a, count in enumerate(counts) for e in range(count)]
    for index, (a, e) in enumerate(order):
        note = arrived[a][e, slots * width :, :].astype(jnp.float32)[0:1, :]
        columns[index : index + 1, :] = note.astype(jnp.int32)
    tell = pltpu.make_async_copy(columns, columns_s, sems.at[2])
    tell.start()
    if hidden:
        gathered[...] = jnp.zeros_like(gathered)
    at_start(load_far.wait)
    for index, (a, e) in enumerate(order):
        _, device = source_of(jnp.int32(index))
        for slot in range(slots):
            products[index * slots + slot] = lax.dot_general(
                arrived[a][e, slot * width : (slot + 1) * width, :],
                far_ref[device * slots + slot],
                NT,
                preferred_element_type=jnp.float32,
            )
    tell.wait()
    if not hidden:
        at_start(load.wait)

    lane_group = lax.broadcasted_iota(jnp.int32, (small, width), 1) // small

    def place_one(index, slot):
        group, device = source_of(index)
        start = group * (own_rows * 2 * chips)
        row = where_ref[device * slots + slot]
        idle = row >= fine_rows
        row = jnp.minimum(row, fine_rows - 1)
        wanted, blocks = distinct(
            [columns_s[index, slot * parts + n] + start for n in range(parts)],
            [products[index * slots + slot, n * small : (n + 1) * small, :] for n in range(parts)],
            unlisted,
        )
        for m in range(parts):
            target = pcols_ref[m, row] - base
            owner, within = target // own_rows, lax.rem(target, own_rows)
            shift = lax.rem(within + parts - m, parts) * small
            here = lane_group == within
            places = []
            for column in wanted:
                s = jnp.where(idle, pattern, slot_of_ref[target, column])
                places.append(pl.ds(pl.multiple_of(s * small, small), small))
            sums = [
                gathered[owner, at, :] + jnp.where(here, pltpu.roll(block, shift, 1), 0.0)
                for at, block in zip(places, blocks)
            ]
            for at, value in zip(places, sums):
                gathered[owner, at, :] = value

    def place_source(index, carry):
        for slot in range(slots):
            place_one(index, slot)
        return carry

    lax.fori_loop(0, total, place_source, 0, unroll=4)

    def end():
        if hidden:
            load.wait()

        def take(owner):
            value = panel[owner, 0:tall, :]
            return value + gathered[owner, 0:tall, :] if hidden else value

        for chip in range(chips):
            send_ref[chip] = take(2 * chip + 1 - core).astype(send_ref.dtype)
            keep_ref[chip] = take(2 * chip + core)

    end() if steps == 1 else pl.when(step == steps - 1)(end)


def add_far(place, where, pcols_t, slot_of, arrived, far, panel, chips):
    steps = 8 if len(arrived) == 2 else 1
    payload, span = arrived[0].shape[1:]
    counts = tuple(one.shape[0] // steps for one in arrived)
    slots, width = far.shape[0], far.shape[1]
    owners, padded, _ = panel.shape
    tall = padded - width // pcols_t.shape[0]
    hbm, smem = pl.BlockSpec(memory_space=pltpu.HBM), pl.BlockSpec(memory_space=pltpu.SMEM)
    outs = ((chips, tall, width), jnp.float32), ((chips, tall, width), jnp.bfloat16)
    held = ((owners, padded, width), jnp.float32)
    scratch = [
        held,
        (far.shape, far.dtype),
        ((slots // steps, width, width), jnp.float32),
        ((sum(counts), span), jnp.int32),
    ]
    scratch_shapes = [pltpu.VMEM(*one) for one in scratch] + [
        pltpu.SMEM((sum(counts), span), jnp.int32),
        pltpu.SemaphoreType.DMA((3,)),
    ]
    if steps == 1:
        scratch_shapes.append(pltpu.VMEM(*held))
        vmem = pl.BlockSpec(memory_space=pltpu.VMEM)
        how = dict(
            in_specs=[smem] * 4 + [hbm, hbm] + [vmem] * len(arrived),
            out_specs=(vmem, vmem),
            scratch_shapes=scratch_shapes,
        )
    else:
        how = dict(
            grid_spec=pltpu.PrefetchScalarGridSpec(
                num_scalar_prefetch=4,
                grid=(steps,),
                in_specs=[hbm, hbm]
                + [pl.BlockSpec((n, payload, span), lambda i, *_: (i, 0, 0)) for n in counts],
                out_specs=tuple(whole(*shape) for shape, _ in outs),
                scratch_shapes=scratch_shapes,
            )
        )
    return pl.pallas_call(
        functools.partial(far_kernel, counts, steps),
        out_shape=tuple(jax.ShapeDtypeStruct(*one) for one in outs),
        compiler_params=pltpu.CompilerParams(vmem_limit_bytes=FAR_MOST if steps == 1 else VMEM_MOST),
        name="add_far",
        **how,
    )(place, where, pcols_t, slot_of, far, panel, *arrived)


def pair_kernel(place_ref, keep_ref, got_ref, mine_ref, *out_refs):
    chips = keep_ref.shape[0]
    chip = place_ref[2]
    mine_ref[...] = keep_ref[chip] + got_ref[chip].astype(jnp.float32)
    for off, out_ref in enumerate(out_refs):
        at = jnp.bitwise_xor(chip, off + 1)
        out_ref[...] = (keep_ref[at] + got_ref[at].astype(jnp.float32)).astype(out_ref.dtype)


def pair(place, keep, got):
    chips, tall, width = keep.shape
    vmem, smem = pl.BlockSpec(memory_space=pltpu.VMEM), pl.BlockSpec(memory_space=pltpu.SMEM)
    return pl.pallas_call(
        pair_kernel,
        out_shape=(jax.ShapeDtypeStruct((tall, width), jnp.float32),)
        + (jax.ShapeDtypeStruct((tall, width), jnp.bfloat16),) * (chips - 1),
        in_specs=[smem, vmem, vmem],
        out_specs=(vmem,) * chips,
        compiler_params=pltpu.CompilerParams(vmem_limit_bytes=room((keep.shape, keep.dtype), (got.shape, got.dtype), *[((tall, width), jnp.float32)] * chips)),
        name="pair",
    )(place, keep, got)


def last_kernel(mine_ref, *refs):
    terms, out_ref = refs[:-1], refs[-1]
    total = mine_ref[...]
    for term in terms:
        total = total + term[...].astype(jnp.float32)
    out_ref[...] = total.T.reshape(out_ref.shape)


def last(mine, terms, own_rows):
    tall, width = mine.shape
    vmem = pl.BlockSpec(memory_space=pltpu.VMEM)
    return pl.pallas_call(
        last_kernel,
        out_shape=jax.ShapeDtypeStruct((own_rows, width // own_rows, tall), jnp.float32),
        in_specs=[vmem] * (1 + len(terms)),
        out_specs=vmem,
        compiler_params=pltpu.CompilerParams(vmem_limit_bytes=room(*[(mine.shape, mine.dtype)] * (3 + len(terms)))),
        name="last",
    )(mine, *terms)


def swap(axis, *arrays):
    return [lax.ppermute(one, axis, [(0, 1), (1, 0)]) for one in arrays]


def local(chips, groups, a_blocks, a_cols, p_rows, p_cols, send_rows, c_cols):
    group_rows, parts = c_cols.shape[0], p_cols.shape[1]
    peers, slot_count = send_rows.shape[1:]
    slots = peers * slot_count
    group, half = lax.axis_index("group"), lax.axis_index("zh")
    chip = lax.axis_index(("zh", "zl"))
    low = lax.axis_index("zl")
    place = jnp.stack(
        [lax.axis_index("core"), group * group_rows, chip, half, jnp.int32(chips), group, low]
    ).astype(jnp.int32)
    wanted, pcols_t = send_rows[0].T, p_cols.T
    sizes = (2 * chips, group_rows * groups, slots)
    rows = a_blocks.shape[0]
    facts = jnp.concatenate([wanted.reshape(-1), pcols_t.reshape(-1)])
    over, facts_over = swap("zh", p_rows, facts)
    scatter = functools.partial(
        lax.all_to_all, axis_name=("group", "zl", "core"), split_axis=0, concat_axis=0, tiled=True
    )
    if chips == 4 and groups == 4:
        beside, facts_beside = swap("core", p_rows, facts)
        *out, pt = pack_two(
            place, facts, facts_beside, p_rows, beside, peers, slot_count, parts
        )
        arrived = out[:1] + [
            lax.ppermute(out[hop], ("group", "zl"), [(q, q ^ hop) for q in range(8)])
            for hop in range(1, 8)
        ]
        over, facts_over, *arrived = lax.optimization_barrier((over, facts_over, *arrived))
    else:
        outgoing, pt = pack(place, facts, p_rows, slot_count, parts)
        arrived = [scatter(outgoing)]
    outgoing, _ = pack(place, facts_over, over, slot_count, parts)
    outgoing, pt = lax.optimization_barrier((outgoing, pt))
    arrived.append(scatter(outgoing))
    panel, far, where, slot_of = near(
        0, rows, place, a_cols, pcols_t, c_cols, pt, a_blocks, *sizes, None
    )
    keep, give = add_far(place, where, pcols_t, slot_of, arrived, far, panel, chips)
    got, = swap("core", give)
    own_rows = group_rows // (2 * chips)
    line = ("zh", "zl")
    if chips == 4:
        mine, *out = pair(place, keep, got)
        terms = [
            lax.ppermute(piece, line, [(q, q ^ (off + 1)) for q in range(chips)])
            for off, piece in enumerate(out)
        ]
        return last(mine, terms, own_rows)
    both = keep + got.astype(jnp.float32)
    mine = lax.dynamic_index_in_dim(both, chip, 0, keepdims=False)
    came = lax.all_to_all(
        both.astype(jnp.bfloat16), line, split_axis=0, concat_axis=0, tiled=True
    ).astype(jnp.float32)
    other = jnp.arange(chips)[:, None, None] != chip
    return last(mine + jnp.sum(jnp.where(other, came, 0.0), 0), [], own_rows)


def solution(mesh):
    groups, ranks = mesh.shape["group"], mesh.shape["rank"]
    chips = ranks // 2
    every = ("group", "zh", "zl", "core")
    fine = Mesh(mesh.devices.reshape(groups, 2, chips // 2, 2), every)
    in_specs = (P(every), P(every), P(every), P(every), P(every), P("group"))
    return jax.shard_map(
        functools.partial(local, chips, groups),
        mesh=fine,
        in_specs=in_specs,
        out_specs=P(every),
        check_vma=False,
    )
```

```python
import functools
import math

import jax
import jax.numpy as jnp
from jax import lax
from jax.experimental import pallas as pl
from jax.experimental.pallas import tpu as pltpu
from jax.sharding import Mesh, PartitionSpec as P

NT = (((1,), (1,)), ((), ()))
NN = (((1,), (0,)), ((), ()))


VMEM_SLACK = 4 << 20
VMEM_MOST = 56 << 20
PACK_MOST = 60 << 20
FAR_MOST = 50 << 20
FIRST_ROWS = 5


def whole(*shape):
    return pl.BlockSpec(shape, lambda *_: (0,) * len(shape))


def room(*arrays):
    return VMEM_SLACK + sum(math.prod(shape) * jnp.dtype(kind).itemsize for shape, kind in arrays)


def flip(rows_ref, unit, row):
    return lax.dot_general(
        unit, rows_ref[row], NT, preferred_element_type=jnp.float32
    ).astype(rows_ref.dtype)


def identity(width, kind):
    row_id = lax.broadcasted_iota(jnp.int32, (width, width), 0)
    col_id = lax.broadcasted_iota(jnp.int32, (width, width), 1)
    return jnp.where(row_id == col_id, 1.0, 0.0).astype(kind)


def pack_kernel(slots, parts, place_ref, facts_ref, p_in, out_ref, *refs):
    *pt_out, p_ref, pt_ref, sems = refs
    load = pltpu.make_async_copy(p_in, p_ref, sems.at[0])
    load.start()
    load.wait()
    rows, span, width = p_ref.shape
    base, half, low = place_ref[1], place_ref[3], place_ref[4]
    unit = identity(width, p_ref.dtype)
    for row in range(rows):
        pt_ref[row] = flip(p_ref, unit, row)
    saves = [pltpu.make_async_copy(pt_ref, one, sems.at[1]) for one in pt_out]
    for save in saves:
        save.start()
    tail = out_ref.shape[1] - slots * width
    lane = lax.broadcasted_iota(jnp.int32, (tail, span), 1)

    def fill(index, carry):
        device = (2 * (index // low) + half) * low + lax.rem(index, low)
        note = jnp.zeros((tail, span), jnp.int32)
        for slot in range(slots):
            row = jnp.maximum(facts_ref[slot, device], 0)
            out_ref[index, slot * width : (slot + 1) * width, :] = pt_ref[row]
            for part in range(parts):
                column = facts_ref[slots + part, row] - base
                note = jnp.where(lane == slot * parts + part, column, note)
        out_ref[index, slots * width :, :] = note.astype(jnp.float32).astype(out_ref.dtype)
        return carry

    lax.fori_loop(0, out_ref.shape[0], fill, 0)
    for save in saves:
        save.wait()


def pack(place, facts, p_rows, slots, parts, keep_flipped):
    rows, span, width = p_rows.shape
    vmem, smem = pl.BlockSpec(memory_space=pltpu.VMEM), pl.BlockSpec(memory_space=pltpu.SMEM)
    kind = p_rows.dtype
    outgoing = (facts.shape[1] // 2, slots * width + 16, span)
    flipped = (rows, width, span)
    hbm = pl.BlockSpec(memory_space=pltpu.HBM)
    kept = 1 if keep_flipped else 0
    return pl.pallas_call(
        functools.partial(pack_kernel, slots, parts),
        out_shape=(jax.ShapeDtypeStruct(outgoing, kind),)
        + (jax.ShapeDtypeStruct(flipped, kind),) * kept,
        in_specs=[smem, smem, hbm],
        out_specs=(vmem,) + (hbm,) * kept,
        scratch_shapes=[
            pltpu.VMEM(p_rows.shape, kind),
            pltpu.VMEM(flipped, kind),
            pltpu.SemaphoreType.DMA((2,)),
        ],
        compiler_params=pltpu.CompilerParams(
            vmem_limit_bytes=PACK_MOST if kept else room((outgoing, kind), *[(flipped, kind)] * 3)
        ),
        name="pack",
    )(place, facts, p_rows)


def distinct(columns, blocks, dump):
    columns, blocks = list(columns), list(blocks)
    for n in range(1, len(columns)):
        again = jnp.bool_(False)
        for before in range(n):
            same = columns[n] == columns[before]
            blocks[before] = blocks[before] + jnp.where(same, blocks[n], 0.0)
            again = again | same
        columns[n] = jnp.where(again, dump, columns[n])
    return columns, blocks


def sources(kind, place_ref, each, step):
    half, low = place_ref[3], place_ref[4]

    def spread(peer, which):
        group = peer // low
        return group, (2 * group + which) * low + lax.rem(peer, low)

    def along(index):
        return spread(index, half)

    def across(index):
        return spread(index, 1 - half)

    def both(index):
        peer = step * each + lax.rem(index, each)
        return spread(peer, jnp.bitwise_xor(half, index // each))

    return {"along": along, "across": across, "both": both}[kind]


def add_slots(
    source_of, pieces, far_ready, panel_ready, place_ref, where_ref, pcols_ref, slot_of_ref,
    far_ref, gathered, products, columns, columns_s, sem,
):
    parts, fine_rows = pcols_ref.shape
    width = far_ref.shape[1]
    small = width // parts
    own_rows = width // small
    base, group_span = place_ref[1], gathered.shape[0] * own_rows
    pattern = gathered.shape[1] // small - 1
    total = len(pieces)
    slots = products.shape[0] // total
    unlisted = slot_of_ref.shape[1] - 1
    for index, (ref, e) in enumerate(pieces):
        note = ref[e, slots * width :, :].astype(jnp.float32)[0:1, :]
        columns[index : index + 1, :] = note.astype(jnp.int32)
    tell = pltpu.make_async_copy(columns, columns_s, sem)
    tell.start()
    far_ready()
    for index, (ref, e) in enumerate(pieces):
        _, device = source_of(jnp.int32(index))
        for slot in range(slots):
            products[index * slots + slot] = lax.dot_general(
                ref[e, slot * width : (slot + 1) * width, :],
                far_ref[device * slots + slot],
                NT,
                preferred_element_type=jnp.float32,
            )
    tell.wait()
    panel_ready()
    lane_group = lax.broadcasted_iota(jnp.int32, (small, width), 1) // small

    def place_one(index, slot):
        group, device = source_of(index)
        start = group * group_span
        row = where_ref[device * slots + slot]
        idle = row >= fine_rows
        row = jnp.minimum(row, fine_rows - 1)
        wanted, blocks = distinct(
            [columns_s[index, slot * parts + n] + start for n in range(parts)],
            [products[index * slots + slot, n * small : (n + 1) * small, :] for n in range(parts)],
            unlisted,
        )
        for m in range(parts):
            target = pcols_ref[m, row] - base
            owner, within = target // own_rows, lax.rem(target, own_rows)
            shift = lax.rem(within + parts - m, parts) * small
            here = lane_group == within
            places = []
            for column in wanted:
                s = jnp.where(idle, pattern, slot_of_ref[target, column])
                places.append(pl.ds(pl.multiple_of(s * small, small), small))
            sums = [
                gathered[owner, at, :] + jnp.where(here, pltpu.roll(block, shift, 1), 0.0)
                for at, block in zip(places, blocks)
            ]
            for at, value in zip(places, sums):
                gathered[owner, at, :] = value

    def place_source(index, carry):
        for slot in range(slots):
            place_one(index, slot)
        return carry

    lax.fori_loop(0, total, place_source, 0, unroll=4)


def near_kernel(
    first_row, hops, place_ref, acols_ref, pcols_ref, ccols_ref, *refs
):
    resumed = hops > 0
    if resumed:
        where_in, slot_of_ref, pt_ref, a_ref, panel_in, far_in = refs[:6]
        came, refs = refs[6 : 6 + hops], refs[6 + hops :]
        panel_out, far_out, where_ref = refs[:3]
        dense, panel, far, weights, products, sems = refs[3:9]
        landed, far_products, notes, notes_s = refs[9:]
    else:
        ctable_ref, pt_ref, a_ref, panel_out, far_out, where_ref, slot_of_ref = refs[:7]
        dense, panel, far, weights, products, sems = refs[7:]
    step, steps = pl.program_id(0), pl.num_programs(0)
    fine_row = step + first_row
    parts, fine_rows = pcols_ref.shape
    block_cols, width = a_ref.shape[1], pt_ref.shape[1]
    span = width // parts
    pattern = ccols_ref.shape[1]
    slots = far_out.shape[0]
    own_rows = width // span
    base = place_ref[1]
    dump = dense.shape[0] // span - 1
    if resumed:
        load_panel = pltpu.make_async_copy(panel_in, panel, sems.at[0])
        load_far = pltpu.make_async_copy(far_in, far.at[pl.ds(0, slots)], sems.at[1])
        land = [
            pltpu.make_async_copy(one, landed.at[at], sems.at[2 + at]) for at, one in enumerate(came)
        ]

    @pl.when(step == 0)
    def _():
        if resumed:
            for one in [load_panel, load_far] + land:
                one.start()
        else:
            panel[...] = jnp.zeros_like(panel)
            far[...] = jnp.zeros_like(far)
            column = lax.broadcasted_iota(jnp.int32, slot_of_ref.shape, 1)
            found = jnp.full(slot_of_ref.shape, pattern, jnp.int32)
            for s in range(pattern):
                found = jnp.where(column == ctable_ref[:, s : s + 1], s, found)
            slot_of_ref[...] = found

        def begin(slot, carry):
            where_ref[slot] = where_in[slot] if resumed else fine_rows
            return carry

        lax.fori_loop(0, slots, begin, 0)

    dense[...] = jnp.zeros_like(dense)
    left = pt_ref[fine_row]
    for k in range(0, block_cols, 2):
        ahead = range(k, min(k + 2, block_cols))
        weighted = lax.dot_general(
            left,
            jnp.concatenate([a_ref[0, j] for j in ahead], axis=1),
            NN,
            preferred_element_type=jnp.float32,
        ).astype(far.dtype)
        for j in ahead:
            weights[j] = weighted[:, (j - k) * width : (j - k + 1) * width]
    for k in range(block_cols):
        source = acols_ref[fine_row, k]
        row = jnp.where(source >= fine_rows, 0, source)
        products[k] = lax.dot_general(
            pt_ref[row], weights[k], NT, preferred_element_type=jnp.float32
        )
    if resumed:

        @pl.when(step == 0)
        def _():
            load_panel.wait()
            load_far.wait()

    for k in range(block_cols):
        source = acols_ref[fine_row, k]
        is_far = source >= fine_rows
        slot = jnp.where(is_far, source - fine_rows, slots)
        far[slot] = weights[k]
        where_ref[slot] = fine_row
        row = jnp.where(is_far, 0, source)
        columns, blocks = distinct(
            [pcols_ref[n, row] for n in range(parts)],
            [products[k, n * span : (n + 1) * span, :] for n in range(parts)],
            dump,
        )
        places = [
            pl.ds(pl.multiple_of(jnp.where(is_far, dump, column) * span, span), span)
            for column in columns
        ]
        sums = [dense[at, :] + block for at, block in zip(places, blocks)]
        for at, value in zip(places, sums):
            dense[at, :] = value

    lane_group = lax.broadcasted_iota(jnp.int32, (span, width), 1) // span
    for m in range(parts):
        row = pcols_ref[m, fine_row] - base
        owner, within = row // own_rows, lax.rem(row, own_rows)
        shift = lax.rem(within + parts - m, parts) * span
        here = lane_group == within
        for first in range(0, pattern, 9):
            chunk = range(first, min(first + 9, pattern))
            sums = []
            for s in chunk:
                at = pl.ds(pl.multiple_of(ccols_ref[row, s] * span, span), span)
                moved = pltpu.roll(dense[at, :], shift, 1)
                sums.append(
                    panel[owner, s * span : (s + 1) * span, :] + jnp.where(here, moved, 0.0)
                )
            for s, value in zip(chunk, sums):
                panel[owner, s * span : (s + 1) * span, :] = value

    @pl.when(step == steps - 1)
    def _():
        if resumed:
            for one in land:
                one.wait()
            add_slots(
                sources("along", place_ref, 1, 0),
                [(landed.at[at], e) for at in range(hops) for e in range(landed.shape[1])],
                lambda: None, lambda: None, place_ref, where_ref, pcols_ref, slot_of_ref,
                far, panel, far_products, notes, notes_s, sems.at[0],
            )
        one = pltpu.make_async_copy(panel, panel_out, sems.at[0])
        two = pltpu.make_async_copy(far.at[pl.ds(0, slots)], far_out, sems.at[1])
        one.start()
        two.start()
        one.wait()
        two.wait()


def near(first_row, rows_here, place, a_cols, pcols_t, c_cols, pt, a_blocks, owners, all_cols, slots, before=None, came=()):
    rows, cols, span, _ = a_blocks.shape
    parts, width = pcols_t.shape[0], pt.shape[1]
    small = width // parts
    group_rows, pattern = c_cols.shape
    tall = (pattern + 1) * small
    hbm, smem = pl.BlockSpec(memory_space=pltpu.HBM), pl.BlockSpec(memory_space=pltpu.SMEM)
    out_shape = [
        jax.ShapeDtypeStruct((owners, tall, width), jnp.float32),
        jax.ShapeDtypeStruct((slots, width, span), jnp.bfloat16),
        jax.ShapeDtypeStruct((slots + 1,), jnp.int32),
    ]
    out_specs = [hbm, hbm, smem]
    in_specs = [
        whole(rows, width, span),
        pl.BlockSpec((1, cols, span, span), lambda i, *_: (i + first_row, 0, 0, 0)),
    ]
    scalars = [place, a_cols, pcols_t, c_cols]
    if before is None:
        in_specs.insert(0, whole(group_rows, pattern))
        operands = [c_cols, pt, a_blocks]
        out_shape.append(jax.ShapeDtypeStruct((group_rows, all_cols + 128), jnp.int32))
        out_specs.append(whole(group_rows, all_cols + 128))
    else:
        scalars += [before[2], before[3]]
        operands = [pt, a_blocks, before[0], before[1], *came]
        in_specs += [hbm, hbm] + [pl.BlockSpec(memory_space=pl.ANY)] * len(came)
    scratch = [
        (((all_cols + 1) * small, width), jnp.float32),
        ((owners, tall, width), jnp.float32),
        ((slots + 1, width, span), jnp.bfloat16),
        ((cols, width, span), jnp.bfloat16),
        ((cols, width, width), jnp.float32),
    ]
    smem_scratch = []
    if before is not None:
        total = len(came) * came[0].shape[0]
        scratch += [
            ((len(came), *came[0].shape), jnp.bfloat16),
            ((slots // 2, width, width), jnp.float32),
            ((total, span), jnp.int32),
        ]
        smem_scratch = [pltpu.SMEM((total, span), jnp.int32)]
    return pl.pallas_call(
        functools.partial(near_kernel, first_row, len(came)),
        out_shape=tuple(out_shape),
        grid_spec=pltpu.PrefetchScalarGridSpec(
            num_scalar_prefetch=len(scalars),
            grid=(rows_here,),
            in_specs=in_specs,
            out_specs=tuple(out_specs),
            scratch_shapes=[pltpu.VMEM(*one) for one in scratch[:5]]
            + [pltpu.SemaphoreType.DMA((2 + len(came),))]
            + [pltpu.VMEM(*one) for one in scratch[5:]]
            + smem_scratch,
        ),
        compiler_params=pltpu.CompilerParams(
            vmem_limit_bytes=VMEM_MOST
        ),
        cost_estimate=pl.CostEstimate(flops=int(1e11), bytes_accessed=int(1e8), transcendentals=0),
        name="near",
    )(*scalars, *operands)


def far_kernel(
    counts, steps, chips, place_ref, where_ref, pcols_ref, slot_of_ref, far_in, panel_in, *refs
):
    arrived, refs = refs[: len(counts)], refs[len(counts) :]
    waves = 2 if steps == 1 else 1
    outs, refs = refs[: 2 * waves], refs[2 * waves :]
    panel, far_ref, products, columns, columns_s, sems, *extra = refs
    hidden = bool(extra)
    gathered = extra[0] if hidden else panel
    step = 0 if steps == 1 else pl.program_id(0)
    tall = outs[0].shape[1]
    core, own_chip = place_ref[0], place_ref[2]
    load = pltpu.make_async_copy(panel_in, panel, sems.at[0])
    load_far = pltpu.make_async_copy(far_in, far_ref, sems.at[1])

    def at_start(action):
        action() if steps == 1 else pl.when(step == 0)(action)

    def begin():
        load_far.start()
        load.start()

    at_start(begin)
    if hidden:
        gathered[...] = jnp.zeros_like(gathered)
    add_slots(
        sources("across" if steps == 1 else "both", place_ref, counts[0], step),
        [(arrived[a], e) for a, count in enumerate(counts) for e in range(count)],
        lambda: at_start(load_far.wait),
        (lambda: None) if hidden else (lambda: at_start(load.wait)),
        place_ref, where_ref, pcols_ref, slot_of_ref, far_ref, gathered,
        products, columns, columns_s, sems.at[2],
    )

    def end():
        if hidden:
            load.wait()

        def take(owner):
            value = panel[owner, 0:tall, :]
            return value + gathered[owner, 0:tall, :] if hidden else value

        for at in range(chips):
            wave, spot = divmod(at, chips // waves)
            send_ref, keep_ref = outs[2 * wave], outs[2 * wave + 1]
            chip = at if waves == 1 else jnp.bitwise_xor(own_chip, chips - 1 - at)
            send_ref[spot] = take(2 * chip + 1 - core).astype(send_ref.dtype)
            keep_ref[spot] = take(2 * chip + core)

    end() if steps == 1 else pl.when(step == steps - 1)(end)


def add_far(place, where, pcols_t, slot_of, arrived, far, panel, chips):
    steps = 8 if len(arrived) == 2 else 1
    waves = 2 if steps == 1 else 1
    payload, span = arrived[0].shape[1:]
    counts = tuple(one.shape[0] // steps for one in arrived)
    width = far.shape[1]
    slot_count = (payload - 16) // width
    owners, padded, _ = panel.shape
    tall = padded - width // pcols_t.shape[0]
    hbm, smem = pl.BlockSpec(memory_space=pltpu.HBM), pl.BlockSpec(memory_space=pltpu.SMEM)
    some = (chips // waves, tall, width)
    outs = ((some, jnp.bfloat16), (some, jnp.float32)) * waves
    held = ((owners, padded, width), jnp.float32)
    scratch = [
        held,
        (far.shape, far.dtype),
        ((sum(counts) * slot_count, width, width), jnp.float32),
        ((sum(counts), span), jnp.int32),
    ]
    scratch_shapes = [pltpu.VMEM(*one) for one in scratch] + [
        pltpu.SMEM((sum(counts), span), jnp.int32),
        pltpu.SemaphoreType.DMA((3,)),
    ]
    if steps == 1:
        scratch_shapes.append(pltpu.VMEM(*held))
        vmem = pl.BlockSpec(memory_space=pltpu.VMEM)
        how = dict(
            in_specs=[smem] * 4 + [hbm, hbm] + [vmem] * len(arrived),
            out_specs=(vmem,) * len(outs),
            scratch_shapes=scratch_shapes,
        )
    else:
        how = dict(
            grid_spec=pltpu.PrefetchScalarGridSpec(
                num_scalar_prefetch=4,
                grid=(steps,),
                in_specs=[hbm, hbm]
                + [pl.BlockSpec((n, payload, span), lambda i, *_: (i, 0, 0)) for n in counts],
                out_specs=tuple(whole(*shape) for shape, _ in outs),
                scratch_shapes=scratch_shapes,
            )
        )
    return pl.pallas_call(
        functools.partial(far_kernel, counts, steps, chips),
        out_shape=tuple(jax.ShapeDtypeStruct(*one) for one in outs),
        compiler_params=pltpu.CompilerParams(vmem_limit_bytes=FAR_MOST if steps == 1 else VMEM_MOST),
        name="add_far",
        **how,
    )(place, where, pcols_t, slot_of, far, panel, *arrived)


def pair_kernel(keep_ref, got_ref, *out_refs):
    for at, out_ref in enumerate(out_refs):
        out_ref[...] = (keep_ref[at] + got_ref[at].astype(jnp.float32)).astype(out_ref.dtype)


def pair(keep, got, kinds):
    _, tall, width = keep.shape
    vmem = pl.BlockSpec(memory_space=pltpu.VMEM)
    return pl.pallas_call(
        pair_kernel,
        out_shape=tuple(jax.ShapeDtypeStruct((tall, width), kind) for kind in kinds),
        in_specs=[vmem, vmem],
        out_specs=(vmem,) * len(kinds),
        compiler_params=pltpu.CompilerParams(
            vmem_limit_bytes=room(
                (keep.shape, keep.dtype), (got.shape, got.dtype), *[((tall, width), jnp.float32)] * 2
            )
        ),
        name="pair",
    )(keep, got)


def last_kernel(mine_ref, *refs):
    terms, out_ref = refs[:-1], refs[-1]
    total = mine_ref[...]
    for term in terms:
        total = total + term[...].astype(jnp.float32)
    out_ref[...] = total.T.reshape(out_ref.shape)


def last(mine, terms, own_rows):
    tall, width = mine.shape
    vmem = pl.BlockSpec(memory_space=pltpu.VMEM)
    return pl.pallas_call(
        last_kernel,
        out_shape=jax.ShapeDtypeStruct((own_rows, width // own_rows, tall), jnp.float32),
        in_specs=[vmem] * (1 + len(terms)),
        out_specs=vmem,
        compiler_params=pltpu.CompilerParams(vmem_limit_bytes=room(*[(mine.shape, mine.dtype)] * (3 + len(terms)))),
        name="last",
    )(mine, *terms)


def swap(axis, *arrays):
    return [lax.ppermute(one, axis, [(0, 1), (1, 0)]) for one in arrays]


def local(chips, groups, a_blocks, a_cols, p_rows, p_cols, send_rows, c_cols):
    group_rows, parts = c_cols.shape[0], p_cols.shape[1]
    peers, slot_count = send_rows.shape[1:]
    slots = peers * slot_count
    group, half = lax.axis_index("group"), lax.axis_index("zh")
    chip = lax.axis_index(("zh", "zl"))
    low = lax.axis_index("zl")
    place = jnp.stack(
        [lax.axis_index("core"), group * group_rows, chip, half, jnp.int32(chips), group, low]
    ).astype(jnp.int32)
    wanted, pcols_t = send_rows[0].T, p_cols.T
    sizes = (2 * chips, group_rows * groups, slots)
    rows = a_blocks.shape[0]
    facts = jnp.concatenate(
        [wanted, jnp.pad(pcols_t, ((0, 0), (0, peers - pcols_t.shape[1])))], axis=0
    )
    over, facts_over = swap("zh", p_rows, facts)
    scatter = functools.partial(
        lax.all_to_all, axis_name=("group", "zl", "core"), split_axis=0, concat_axis=0, tiled=True
    )
    across = functools.partial(pack, place, slots=slot_count, parts=parts)
    shared = (place, a_cols, pcols_t, c_cols)
    outgoing, pt = across(facts, p_rows, keep_flipped=True)
    came = [scatter(outgoing)]
    if chips == 4:
        before = near(0, FIRST_ROWS, *shared, pt, a_blocks, *sizes)
        over, facts_over, before = lax.optimization_barrier((over, facts_over, before))
        outgoing, = across(facts_over, over, keep_flipped=False)
        outgoing, before = lax.optimization_barrier((outgoing, before))
        arrived = [scatter(outgoing)]
        panel, far, where = near(
            FIRST_ROWS, rows - FIRST_ROWS, *shared, pt, a_blocks, *sizes, before, came
        )
        slot_of = before[3]
    else:
        arrived = came + [scatter(across(facts_over, over, keep_flipped=False)[0])]
        panel, far, where, slot_of = near(0, rows, *shared, pt, a_blocks, *sizes)
    sums = add_far(place, where, pcols_t, slot_of, arrived, far, panel, chips)
    own_rows = group_rows // (2 * chips)
    line = ("zh", "zl")
    if chips == 4:
        give, keep, give_late, keep_late = sums
        got, = swap("core", give)
        out = pair(keep, got, (jnp.bfloat16,) * 2)
        give_late, keep_late, *out = lax.optimization_barrier((give_late, keep_late, *out))
        got_late, = swap("core", give_late)
        out_late, mine = pair(keep_late, got_late, (jnp.bfloat16, jnp.float32))
        terms = [
            lax.ppermute(piece, line, [(q, q ^ off) for q in range(chips)])
            for off, piece in zip((3, 2, 1), [*out, out_late])
        ]
        return last(mine, terms, own_rows)
    give, keep = sums
    got, = swap("core", give)
    both = keep + got.astype(jnp.float32)
    mine = lax.dynamic_index_in_dim(both, chip, 0, keepdims=False)
    came = lax.all_to_all(
        both.astype(jnp.bfloat16), line, split_axis=0, concat_axis=0, tiled=True
    ).astype(jnp.float32)
    other = jnp.arange(chips)[:, None, None] != chip
    return last(mine + jnp.sum(jnp.where(other, came, 0.0), 0), [], own_rows)


def solution(mesh):
    groups, ranks = mesh.shape["group"], mesh.shape["rank"]
    chips = ranks // 2
    every = ("group", "zh", "zl", "core")
    fine = Mesh(mesh.devices.reshape(groups, 2, chips // 2, 2), every)
    in_specs = (P(every), P(every), P(every), P(every), P(every), P("group"))
    return jax.shard_map(
        functools.partial(local, chips, groups),
        mesh=fine,
        in_specs=in_specs,
        out_specs=P(every),
        check_vma=False,
    )
```

```python
import functools
import math

import jax
import jax.numpy as jnp
from jax import lax
from jax.experimental import pallas as pl
from jax.experimental.pallas import tpu as pltpu
from jax.sharding import Mesh, PartitionSpec as P

NT = (((1,), (1,)), ((), ()))
NN = (((1,), (0,)), ((), ()))


VMEM_SLACK = 4 << 20
VMEM_MOST = 56 << 20
PACK_MOST = 60 << 20
FAR_MOST = 50 << 20
FIRST_ROWS = 6


def whole(*shape):
    return pl.BlockSpec(shape, lambda *_: (0,) * len(shape))


def room(*arrays):
    return VMEM_SLACK + sum(math.prod(shape) * jnp.dtype(kind).itemsize for shape, kind in arrays)


def flip(rows_ref, unit, row):
    return lax.dot_general(
        unit, rows_ref[row], NT, preferred_element_type=jnp.float32
    ).astype(rows_ref.dtype)


def identity(width, kind):
    row_id = lax.broadcasted_iota(jnp.int32, (width, width), 0)
    col_id = lax.broadcasted_iota(jnp.int32, (width, width), 1)
    return jnp.where(row_id == col_id, 1.0, 0.0).astype(kind)


def pack_kernel(slots, parts, place_ref, facts_ref, p_in, out_ref, *refs):
    *pt_out, p_ref, pt_ref, sems = refs
    load = pltpu.make_async_copy(p_in, p_ref, sems.at[0])
    load.start()
    load.wait()
    rows, span, width = p_ref.shape
    base, half, low = place_ref[1], place_ref[3], place_ref[4]
    unit = identity(width, p_ref.dtype)
    for row in range(rows):
        pt_ref[row] = flip(p_ref, unit, row)
    saves = [pltpu.make_async_copy(pt_ref, one, sems.at[1]) for one in pt_out]
    for save in saves:
        save.start()
    tail = out_ref.shape[1] - slots * width
    lane = lax.broadcasted_iota(jnp.int32, (tail, span), 1)

    def fill(index, carry):
        device = (2 * (index // low) + half) * low + lax.rem(index, low)
        note = jnp.zeros((tail, span), jnp.int32)
        for slot in range(slots):
            row = jnp.maximum(facts_ref[slot, device], 0)
            out_ref[index, slot * width : (slot + 1) * width, :] = pt_ref[row]
            for part in range(parts):
                column = facts_ref[slots + part, row] - base
                note = jnp.where(lane == slot * parts + part, column, note)
        out_ref[index, slots * width :, :] = note.astype(jnp.float32).astype(out_ref.dtype)
        return carry

    lax.fori_loop(0, out_ref.shape[0], fill, 0)
    for save in saves:
        save.wait()


def pack(place, facts, p_rows, slots, parts, keep_flipped):
    rows, span, width = p_rows.shape
    vmem, smem = pl.BlockSpec(memory_space=pltpu.VMEM), pl.BlockSpec(memory_space=pltpu.SMEM)
    kind = p_rows.dtype
    outgoing = (facts.shape[1] // 2, slots * width + 16, span)
    flipped = (rows, width, span)
    hbm = pl.BlockSpec(memory_space=pltpu.HBM)
    kept = 1 if keep_flipped else 0
    return pl.pallas_call(
        functools.partial(pack_kernel, slots, parts),
        out_shape=(jax.ShapeDtypeStruct(outgoing, kind),)
        + (jax.ShapeDtypeStruct(flipped, kind),) * kept,
        in_specs=[smem, smem, hbm],
        out_specs=(vmem,) + (hbm,) * kept,
        scratch_shapes=[
            pltpu.VMEM(p_rows.shape, kind),
            pltpu.VMEM(flipped, kind),
            pltpu.SemaphoreType.DMA((2,)),
        ],
        compiler_params=pltpu.CompilerParams(
            vmem_limit_bytes=PACK_MOST if kept else room((outgoing, kind), *[(flipped, kind)] * 3)
        ),
        name="pack",
    )(place, facts, p_rows)


def distinct(columns, blocks, dump):
    columns, blocks = list(columns), list(blocks)
    for n in range(1, len(columns)):
        again = jnp.bool_(False)
        for before in range(n):
            same = columns[n] == columns[before]
            blocks[before] = blocks[before] + jnp.where(same, blocks[n], 0.0)
            again = again | same
        columns[n] = jnp.where(again, dump, columns[n])
    return columns, blocks


def sources(kind, place_ref, each, step):
    half, low = place_ref[3], place_ref[4]

    def spread(peer, which):
        group = peer // low
        return group, (2 * group + which) * low + lax.rem(peer, low)

    def along(index):
        return spread(index, half)

    def across(index):
        return spread(index, 1 - half)

    def both(index):
        peer = step * each + lax.rem(index, each)
        return spread(peer, jnp.bitwise_xor(half, index // each))

    return {"along": along, "across": across, "both": both}[kind]


def add_slots(
    source_of, pieces, far_ready, panel_ready, place_ref, where_ref, pcols_ref, slot_of_ref,
    far_ref, gathered, products, columns, columns_s, sem,
):
    parts, fine_rows = pcols_ref.shape
    width = far_ref.shape[1]
    small = width // parts
    own_rows = width // small
    base, group_span = place_ref[1], gathered.shape[0] * own_rows
    pattern = gathered.shape[1] // small - 1
    total = len(pieces)
    slots = products.shape[0] // total
    unlisted = slot_of_ref.shape[1] - 1
    for index, (ref, e) in enumerate(pieces):
        note = ref[e, slots * width :, :].astype(jnp.float32)[0:1, :]
        columns[index : index + 1, :] = note.astype(jnp.int32)
    tell = pltpu.make_async_copy(columns, columns_s, sem)
    tell.start()
    far_ready()
    for index, (ref, e) in enumerate(pieces):
        _, device = source_of(jnp.int32(index))
        for slot in range(slots):
            products[index * slots + slot] = lax.dot_general(
                ref[e, slot * width : (slot + 1) * width, :],
                far_ref[device * slots + slot],
                NT,
                preferred_element_type=jnp.float32,
            )
    tell.wait()
    panel_ready()
    lane_group = lax.broadcasted_iota(jnp.int32, (small, width), 1) // small

    def place_one(index, slot):
        group, device = source_of(index)
        start = group * group_span
        row = where_ref[device * slots + slot]
        idle = row >= fine_rows
        row = jnp.minimum(row, fine_rows - 1)
        wanted, blocks = distinct(
            [columns_s[index, slot * parts + n] + start for n in range(parts)],
            [products[index * slots + slot, n * small : (n + 1) * small, :] for n in range(parts)],
            unlisted,
        )
        for m in range(parts):
            target = pcols_ref[m, row] - base
            owner, within = target // own_rows, lax.rem(target, own_rows)
            shift = lax.rem(within + parts - m, parts) * small
            here = lane_group == within
            places = []
            for column in wanted:
                s = jnp.where(idle, pattern, slot_of_ref[target, column])
                places.append(pl.ds(pl.multiple_of(s * small, small), small))
            sums = [
                gathered[owner, at, :] + jnp.where(here, pltpu.roll(block, shift, 1), 0.0)
                for at, block in zip(places, blocks)
            ]
            for at, value in zip(places, sums):
                gathered[owner, at, :] = value

    def place_source(index, carry):
        for slot in range(slots):
            place_one(index, slot)
        return carry

    lax.fori_loop(0, total, place_source, 0, unroll=16)


def near_kernel(
    first_row, hops, place_ref, acols_ref, pcols_ref, ccols_ref, *refs
):
    resumed = hops > 0
    if resumed:
        where_in, slot_of_ref, pt_ref, a_ref, panel_in, far_in = refs[:6]
        came, refs = refs[6 : 6 + hops], refs[6 + hops :]
        panel_out, far_out, where_ref = refs[:3]
        dense, panel, far, weights, products, sems = refs[3:9]
        landed, far_products, notes, notes_s = refs[9:]
    else:
        ctable_ref, pt_ref, a_ref, panel_out, far_out, where_ref, slot_of_ref = refs[:7]
        dense, panel, far, weights, products, sems = refs[7:]
    step, steps = pl.program_id(0), pl.num_programs(0)
    fine_row = step + first_row
    parts, fine_rows = pcols_ref.shape
    block_cols, width = a_ref.shape[1], pt_ref.shape[1]
    span = width // parts
    pattern = ccols_ref.shape[1]
    slots = far_out.shape[0]
    own_rows = width // span
    base = place_ref[1]
    dump = dense.shape[0] // span - 1
    if resumed:
        load_panel = pltpu.make_async_copy(panel_in, panel, sems.at[0])
        load_far = pltpu.make_async_copy(far_in, far.at[pl.ds(0, slots)], sems.at[1])
        land = [
            pltpu.make_async_copy(one, landed.at[at], sems.at[2 + at]) for at, one in enumerate(came)
        ]

    @pl.when(step == 0)
    def _():
        if resumed:
            for one in [load_panel, load_far] + land:
                one.start()
        else:
            panel[...] = jnp.zeros_like(panel)
            far[...] = jnp.zeros_like(far)
            column = lax.broadcasted_iota(jnp.int32, slot_of_ref.shape, 1)
            found = jnp.full(slot_of_ref.shape, pattern, jnp.int32)
            for s in range(pattern):
                found = jnp.where(column == ctable_ref[:, s : s + 1], s, found)
            slot_of_ref[...] = found

        def begin(slot, carry):
            where_ref[slot] = where_in[slot] if resumed else fine_rows
            return carry

        lax.fori_loop(0, slots, begin, 0)

    dense[...] = jnp.zeros_like(dense)
    left = pt_ref[fine_row]
    for k in range(0, block_cols, 2):
        ahead = range(k, min(k + 2, block_cols))
        weighted = lax.dot_general(
            left,
            jnp.concatenate([a_ref[0, j] for j in ahead], axis=1),
            NN,
            preferred_element_type=jnp.float32,
        ).astype(far.dtype)
        for j in ahead:
            weights[j] = weighted[:, (j - k) * width : (j - k + 1) * width]
    for k in range(block_cols):
        source = acols_ref[fine_row, k]
        row = jnp.where(source >= fine_rows, 0, source)
        products[k] = lax.dot_general(
            pt_ref[row], weights[k], NT, preferred_element_type=jnp.float32
        )
    if resumed:

        @pl.when(step == 0)
        def _():
            load_panel.wait()
            load_far.wait()

    for k in range(block_cols):
        source = acols_ref[fine_row, k]
        is_far = source >= fine_rows
        slot = jnp.where(is_far, source - fine_rows, slots)
        far[slot] = weights[k]
        where_ref[slot] = fine_row
        row = jnp.where(is_far, 0, source)
        columns, blocks = distinct(
            [pcols_ref[n, row] for n in range(parts)],
            [products[k, n * span : (n + 1) * span, :] for n in range(parts)],
            dump,
        )
        places = [
            pl.ds(pl.multiple_of(jnp.where(is_far, dump, column) * span, span), span)
            for column in columns
        ]
        sums = [dense[at, :] + block for at, block in zip(places, blocks)]
        for at, value in zip(places, sums):
            dense[at, :] = value

    lane_group = lax.broadcasted_iota(jnp.int32, (span, width), 1) // span
    for m in range(parts):
        row = pcols_ref[m, fine_row] - base
        owner, within = row // own_rows, lax.rem(row, own_rows)
        shift = lax.rem(within + parts - m, parts) * span
        here = lane_group == within
        for first in range(0, pattern, 9):
            chunk = range(first, min(first + 9, pattern))
            sums = []
            for s in chunk:
                at = pl.ds(pl.multiple_of(ccols_ref[row, s] * span, span), span)
                moved = pltpu.roll(dense[at, :], shift, 1)
                sums.append(
                    panel[owner, s * span : (s + 1) * span, :] + jnp.where(here, moved, 0.0)
                )
            for s, value in zip(chunk, sums):
                panel[owner, s * span : (s + 1) * span, :] = value

    @pl.when(step == steps - 1)
    def _():
        if resumed:
            for one in land:
                one.wait()
            add_slots(
                sources("along", place_ref, 1, 0),
                [(landed.at[at], e) for at in range(hops) for e in range(landed.shape[1])],
                lambda: None, lambda: None, place_ref, where_ref, pcols_ref, slot_of_ref,
                far, panel, far_products, notes, notes_s, sems.at[0],
            )
        one = pltpu.make_async_copy(panel, panel_out, sems.at[0])
        two = pltpu.make_async_copy(far.at[pl.ds(0, slots)], far_out, sems.at[1])
        one.start()
        two.start()
        one.wait()
        two.wait()


def near(first_row, rows_here, place, a_cols, pcols_t, c_cols, pt, a_blocks, owners, all_cols, slots, before=None, came=()):
    rows, cols, span, _ = a_blocks.shape
    parts, width = pcols_t.shape[0], pt.shape[1]
    small = width // parts
    group_rows, pattern = c_cols.shape
    tall = (pattern + 1) * small
    hbm, smem = pl.BlockSpec(memory_space=pltpu.HBM), pl.BlockSpec(memory_space=pltpu.SMEM)
    out_shape = [
        jax.ShapeDtypeStruct((owners, tall, width), jnp.float32),
        jax.ShapeDtypeStruct((slots, width, span), jnp.bfloat16),
        jax.ShapeDtypeStruct((slots + 1,), jnp.int32),
    ]
    out_specs = [hbm, hbm, smem]
    in_specs = [
        whole(rows, width, span),
        pl.BlockSpec((1, cols, span, span), lambda i, *_: (i + first_row, 0, 0, 0)),
    ]
    scalars = [place, a_cols, pcols_t, c_cols]
    if before is None:
        in_specs.insert(0, whole(group_rows, pattern))
        operands = [c_cols, pt, a_blocks]
        out_shape.append(jax.ShapeDtypeStruct((group_rows, all_cols + 128), jnp.int32))
        out_specs.append(whole(group_rows, all_cols + 128))
    else:
        scalars += [before[2], before[3]]
        operands = [pt, a_blocks, before[0], before[1], *came]
        in_specs += [hbm, hbm] + [pl.BlockSpec(memory_space=pl.ANY)] * len(came)
    scratch = [
        (((all_cols + 1) * small, width), jnp.float32),
        ((owners, tall, width), jnp.float32),
        ((slots + 1, width, span), jnp.bfloat16),
        ((cols, width, span), jnp.bfloat16),
        ((cols, width, width), jnp.float32),
    ]
    smem_scratch = []
    if before is not None:
        total = len(came) * came[0].shape[0]
        scratch += [
            ((len(came), *came[0].shape), jnp.bfloat16),
            ((slots // 2, width, width), jnp.float32),
            ((total, span), jnp.int32),
        ]
        smem_scratch = [pltpu.SMEM((total, span), jnp.int32)]
    return pl.pallas_call(
        functools.partial(near_kernel, first_row, len(came)),
        out_shape=tuple(out_shape),
        grid_spec=pltpu.PrefetchScalarGridSpec(
            num_scalar_prefetch=len(scalars),
            grid=(rows_here,),
            in_specs=in_specs,
            out_specs=tuple(out_specs),
            scratch_shapes=[pltpu.VMEM(*one) for one in scratch[:5]]
            + [pltpu.SemaphoreType.DMA((2 + len(came),))]
            + [pltpu.VMEM(*one) for one in scratch[5:]]
            + smem_scratch,
        ),
        compiler_params=pltpu.CompilerParams(
            vmem_limit_bytes=VMEM_MOST
        ),
        cost_estimate=pl.CostEstimate(flops=int(1e11), bytes_accessed=int(1e8), transcendentals=0),
        name="near",
    )(*scalars, *operands)


def far_kernel(
    counts, steps, chips, place_ref, where_in, pcols_ref, slot_of_ref, far_in, panel_in, *refs
):
    arrived, refs = refs[: len(counts)], refs[len(counts) :]
    waves = 2 if steps == 1 else 1
    outs, refs = refs[: 2 * waves], refs[2 * waves :]
    panel, far_ref, products, columns, columns_s, sems, *extra = refs
    if steps == 1:
        where_ref, *extra = extra
    hidden = bool(extra)
    gathered = extra[0] if hidden else panel
    step = 0 if steps == 1 else pl.program_id(0)
    tall = outs[0].shape[1]
    core, own_chip = place_ref[0], place_ref[2]
    load = pltpu.make_async_copy(panel_in, panel, sems.at[0])
    if steps == 1:
        slots = products.shape[0] // counts[0]
        group_count = counts[0] // chips
        spans = [
            pl.ds(pl.multiple_of((2 * group + 1 - place_ref[3]) * slots * chips, 8), slots * chips)
            for group in range(group_count)
        ]
        loads = [
            pltpu.make_async_copy(far_in.at[one], far_ref.at[one], sems.at[4 + at])
            for at, one in enumerate(spans)
        ]
        loads.append(pltpu.make_async_copy(where_in, where_ref, sems.at[3]))
    else:
        where_ref = where_in
        loads = [pltpu.make_async_copy(far_in, far_ref, sems.at[1])]

    def far_ready():
        for one in loads:
            one.wait()

    def at_start(action):
        action() if steps == 1 else pl.when(step == 0)(action)

    def begin():
        for one in loads:
            one.start()
        load.start()

    at_start(begin)
    if hidden:
        gathered[...] = jnp.zeros_like(gathered)
    add_slots(
        sources("across" if steps == 1 else "both", place_ref, counts[0], step),
        [(arrived[a], e) for a, count in enumerate(counts) for e in range(count)],
        lambda: at_start(far_ready),
        (lambda: None) if hidden else (lambda: at_start(load.wait)),
        place_ref, where_ref, pcols_ref, slot_of_ref, far_ref, gathered,
        products, columns, columns_s, sems.at[2],
    )

    def end():
        if hidden:
            load.wait()

        def take(owner):
            value = panel[owner, 0:tall, :]
            return value + gathered[owner, 0:tall, :] if hidden else value

        for at in range(chips):
            wave, spot = divmod(at, chips // waves)
            send_ref, keep_ref = outs[2 * wave], outs[2 * wave + 1]
            chip = at if waves == 1 else jnp.bitwise_xor(own_chip, chips - 1 - at)
            send_ref[spot] = take(2 * chip + 1 - core).astype(send_ref.dtype)
            keep_ref[spot] = take(2 * chip + core)

    end() if steps == 1 else pl.when(step == steps - 1)(end)


def add_far(place, where, pcols_t, slot_of, arrived, far, panel, chips):
    steps = 8 if len(arrived) == 2 else 1
    waves = 2 if steps == 1 else 1
    payload, span = arrived[0].shape[1:]
    counts = tuple(one.shape[0] // steps for one in arrived)
    width = far.shape[1]
    slot_count = (payload - 16) // width
    owners, padded, _ = panel.shape
    tall = padded - width // pcols_t.shape[0]
    hbm, smem = pl.BlockSpec(memory_space=pltpu.HBM), pl.BlockSpec(memory_space=pltpu.SMEM)
    some = (chips // waves, tall, width)
    outs = ((some, jnp.bfloat16), (some, jnp.float32)) * waves
    held = ((owners, padded, width), jnp.float32)
    scratch = [
        held,
        (far.shape, far.dtype),
        ((sum(counts) * slot_count, width, width), jnp.float32),
        ((sum(counts), span), jnp.int32),
    ]
    scratch_shapes = [pltpu.VMEM(*one) for one in scratch] + [
        pltpu.SMEM((sum(counts), span), jnp.int32),
        pltpu.SemaphoreType.DMA((8,)),
    ]
    if steps == 1:
        scratch_shapes.append(pltpu.SMEM(where.shape, where.dtype))
        vmem = pl.BlockSpec(memory_space=pltpu.VMEM)
        how = dict(
            in_specs=[smem, hbm, smem, smem, hbm, hbm] + [vmem] * len(arrived),
            out_specs=(vmem,) * len(outs),
            scratch_shapes=scratch_shapes,
        )
    else:
        how = dict(
            grid_spec=pltpu.PrefetchScalarGridSpec(
                num_scalar_prefetch=4,
                grid=(steps,),
                in_specs=[hbm, hbm]
                + [pl.BlockSpec((n, payload, span), lambda i, *_: (i, 0, 0)) for n in counts],
                out_specs=tuple(whole(*shape) for shape, _ in outs),
                scratch_shapes=scratch_shapes,
            )
        )
    return pl.pallas_call(
        functools.partial(far_kernel, counts, steps, chips),
        out_shape=tuple(jax.ShapeDtypeStruct(*one) for one in outs),
        compiler_params=pltpu.CompilerParams(vmem_limit_bytes=FAR_MOST if steps == 1 else VMEM_MOST),
        name="add_far",
        **how,
    )(place, where, pcols_t, slot_of, far, panel, *arrived)


def pair_kernel(keep_ref, got_ref, *out_refs):
    for at, out_ref in enumerate(out_refs):
        out_ref[...] = (keep_ref[at] + got_ref[at].astype(jnp.float32)).astype(out_ref.dtype)


def pair(keep, got, kinds):
    _, tall, width = keep.shape
    vmem = pl.BlockSpec(memory_space=pltpu.VMEM)
    return pl.pallas_call(
        pair_kernel,
        out_shape=tuple(jax.ShapeDtypeStruct((tall, width), kind) for kind in kinds),
        in_specs=[vmem, vmem],
        out_specs=(vmem,) * len(kinds),
        compiler_params=pltpu.CompilerParams(
            vmem_limit_bytes=room(
                (keep.shape, keep.dtype), (got.shape, got.dtype), *[((tall, width), jnp.float32)] * 2
            )
        ),
        name="pair",
    )(keep, got)


def last_kernel(mine_ref, *refs):
    terms, out_ref = refs[:-1], refs[-1]
    total = mine_ref[...]
    for term in terms:
        total = total + term[...].astype(jnp.float32)
    out_ref[...] = total.T.reshape(out_ref.shape)


def last(mine, terms, own_rows):
    tall, width = mine.shape
    vmem = pl.BlockSpec(memory_space=pltpu.VMEM)
    return pl.pallas_call(
        last_kernel,
        out_shape=jax.ShapeDtypeStruct((own_rows, width // own_rows, tall), jnp.float32),
        in_specs=[vmem] * (1 + len(terms)),
        out_specs=vmem,
        compiler_params=pltpu.CompilerParams(vmem_limit_bytes=room(*[(mine.shape, mine.dtype)] * (3 + len(terms)))),
        name="last",
    )(mine, *terms)


def swap(axis, *arrays):
    return [lax.ppermute(one, axis, [(0, 1), (1, 0)]) for one in arrays]


def local(chips, groups, a_blocks, a_cols, p_rows, p_cols, send_rows, c_cols):
    group_rows, parts = c_cols.shape[0], p_cols.shape[1]
    peers, slot_count = send_rows.shape[1:]
    slots = peers * slot_count
    group, half = lax.axis_index("group"), lax.axis_index("zh")
    chip = lax.axis_index(("zh", "zl"))
    low = lax.axis_index("zl")
    place = jnp.stack(
        [lax.axis_index("core"), group * group_rows, chip, half, jnp.int32(chips), group, low]
    ).astype(jnp.int32)
    wanted, pcols_t = send_rows[0].T, p_cols.T
    sizes = (2 * chips, group_rows * groups, slots)
    rows = a_blocks.shape[0]
    facts = jnp.concatenate(
        [wanted, jnp.pad(pcols_t, ((0, 0), (0, peers - pcols_t.shape[1])))], axis=0
    )
    over, facts_over = swap("zh", p_rows, facts)
    scatter = functools.partial(
        lax.all_to_all, axis_name=("group", "zl", "core"), split_axis=0, concat_axis=0, tiled=True
    )
    across = functools.partial(pack, place, slots=slot_count, parts=parts)
    shared = (place, a_cols, pcols_t, c_cols)
    outgoing, pt = across(facts, p_rows, keep_flipped=True)
    came = [scatter(outgoing)]
    if chips == 4:
        before = near(0, FIRST_ROWS, *shared, pt, a_blocks, *sizes)
        over, facts_over, before = lax.optimization_barrier((over, facts_over, before))
        outgoing, = across(facts_over, over, keep_flipped=False)
        outgoing, before = lax.optimization_barrier((outgoing, before))
        arrived = [scatter(outgoing)]
        panel, far, where = near(
            FIRST_ROWS, rows - FIRST_ROWS, *shared, pt, a_blocks, *sizes, before, came
        )
        slot_of = before[3]
    else:
        arrived = came + [scatter(across(facts_over, over, keep_flipped=False)[0])]
        panel, far, where, slot_of = near(0, rows, *shared, pt, a_blocks, *sizes)
    sums = add_far(place, where, pcols_t, slot_of, arrived, far, panel, chips)
    own_rows = group_rows // (2 * chips)
    line = ("zh", "zl")
    if chips == 4:
        give, keep, give_late, keep_late = sums
        got, = swap("core", give)
        out = pair(keep, got, (jnp.bfloat16,) * 2)
        give_late, keep_late, *out = lax.optimization_barrier((give_late, keep_late, *out))
        got_late, = swap("core", give_late)
        out_late, mine = pair(keep_late, got_late, (jnp.bfloat16, jnp.float32))
        terms = [
            lax.ppermute(piece, line, [(q, q ^ off) for q in range(chips)])
            for off, piece in zip((3, 2, 1), [*out, out_late])
        ]
        return last(mine, terms, own_rows)
    give, keep = sums
    got, = swap("core", give)
    both = keep + got.astype(jnp.float32)
    mine = lax.dynamic_index_in_dim(both, chip, 0, keepdims=False)
    came = lax.all_to_all(
        both.astype(jnp.bfloat16), line, split_axis=0, concat_axis=0, tiled=True
    ).astype(jnp.float32)
    other = jnp.arange(chips)[:, None, None] != chip
    return last(mine + jnp.sum(jnp.where(other, came, 0.0), 0), [], own_rows)


def solution(mesh):
    groups, ranks = mesh.shape["group"], mesh.shape["rank"]
    chips = ranks // 2
    every = ("group", "zh", "zl", "core")
    fine = Mesh(mesh.devices.reshape(groups, 2, chips // 2, 2), every)
    in_specs = (P(every), P(every), P(every), P(every), P(every), P("group"))
    return jax.shard_map(
        functools.partial(local, chips, groups),
        mesh=fine,
        in_specs=in_specs,
        out_specs=P(every),
        check_vma=False,
    )
```

```python
import functools
import math

import jax
import jax.numpy as jnp
from jax import lax
from jax.experimental import pallas as pl
from jax.experimental.pallas import tpu as pltpu
from jax.sharding import Mesh, PartitionSpec as P

NT = (((1,), (1,)), ((), ()))
NN = (((1,), (0,)), ((), ()))


VMEM_SLACK = 4 << 20
VMEM_MOST = 56 << 20
PACK_MOST = 60 << 20
FAR_MOST = 50 << 20
FIRST_ROWS = 6


def whole(*shape):
    return pl.BlockSpec(shape, lambda *_: (0,) * len(shape))


def room(*arrays):
    return VMEM_SLACK + sum(math.prod(shape) * jnp.dtype(kind).itemsize for shape, kind in arrays)


def flip(rows_ref, unit, row):
    return lax.dot_general(
        unit, rows_ref[row], NT, preferred_element_type=jnp.float32
    ).astype(rows_ref.dtype)


def identity(width, kind):
    row_id = lax.broadcasted_iota(jnp.int32, (width, width), 0)
    col_id = lax.broadcasted_iota(jnp.int32, (width, width), 1)
    return jnp.where(row_id == col_id, 1.0, 0.0).astype(kind)


def pack_kernel(slots, parts, place_ref, facts_ref, p_in, out_ref, *refs):
    *pt_out, p_ref, pt_ref, sems = refs
    load = pltpu.make_async_copy(p_in, p_ref, sems.at[0])
    load.start()
    load.wait()
    rows, span, width = p_ref.shape
    base, half, low = place_ref[1], place_ref[3], place_ref[4]
    unit = identity(width, p_ref.dtype)
    for row in range(rows):
        pt_ref[row] = flip(p_ref, unit, row)
    saves = [pltpu.make_async_copy(pt_ref, one, sems.at[1]) for one in pt_out]
    for save in saves:
        save.start()
    tail = out_ref.shape[1] - slots * width
    lane = lax.broadcasted_iota(jnp.int32, (tail, span), 1)

    def fill(index, carry):
        device = (2 * (index // low) + half) * low + lax.rem(index, low)
        note = jnp.zeros((tail, span), jnp.int32)
        for slot in range(slots):
            row = jnp.maximum(facts_ref[slot, device], 0)
            out_ref[index, slot * width : (slot + 1) * width, :] = pt_ref[row]
            for part in range(parts):
                column = facts_ref[slots + part, row] - base
                note = jnp.where(lane == slot * parts + part, column, note)
        out_ref[index, slots * width :, :] = note.astype(jnp.float32).astype(out_ref.dtype)
        return carry

    lax.fori_loop(0, out_ref.shape[0], fill, 0)
    for save in saves:
        save.wait()


def pack(place, facts, p_rows, slots, parts, keep_flipped):
    rows, span, width = p_rows.shape
    vmem, smem = pl.BlockSpec(memory_space=pltpu.VMEM), pl.BlockSpec(memory_space=pltpu.SMEM)
    kind = p_rows.dtype
    outgoing = (facts.shape[1] // 2, slots * width + 16, span)
    flipped = (rows, width, span)
    hbm = pl.BlockSpec(memory_space=pltpu.HBM)
    kept = 1 if keep_flipped else 0
    return pl.pallas_call(
        functools.partial(pack_kernel, slots, parts),
        out_shape=(jax.ShapeDtypeStruct(outgoing, kind),)
        + (jax.ShapeDtypeStruct(flipped, kind),) * kept,
        in_specs=[smem, smem, hbm],
        out_specs=(vmem,) + (hbm,) * kept,
        scratch_shapes=[
            pltpu.VMEM(p_rows.shape, kind),
            pltpu.VMEM(flipped, kind),
            pltpu.SemaphoreType.DMA((2,)),
        ],
        compiler_params=pltpu.CompilerParams(
            vmem_limit_bytes=PACK_MOST if kept else room((outgoing, kind), *[(flipped, kind)] * 3)
        ),
        name="pack",
    )(place, facts, p_rows)


def distinct(columns, blocks, dump):
    columns, blocks = list(columns), list(blocks)
    for n in range(1, len(columns)):
        again = jnp.bool_(False)
        for before in range(n):
            same = columns[n] == columns[before]
            blocks[before] = blocks[before] + jnp.where(same, blocks[n], 0.0)
            again = again | same
        columns[n] = jnp.where(again, dump, columns[n])
    return columns, blocks


def sources(kind, place_ref, each, step):
    half, low = place_ref[3], place_ref[4]

    def spread(peer, which):
        group = peer // low
        return group, (2 * group + which) * low + lax.rem(peer, low)

    def along(index):
        return spread(index, half)

    def across(index):
        return spread(index, 1 - half)

    def both(index):
        peer = step * each + lax.rem(index, each)
        return spread(peer, jnp.bitwise_xor(half, index // each))

    return {"along": along, "across": across, "both": both}[kind]


def add_slots(
    source_of, pieces, far_ready, panel_ready, place_ref, where_ref, pcols_ref, slot_of_ref,
    far_ref, gathered, products, columns, columns_s, sem,
):
    parts, fine_rows = pcols_ref.shape
    width = far_ref.shape[1]
    small = width // parts
    own_rows = width // small
    base, group_span = place_ref[1], gathered.shape[0] * own_rows
    pattern = gathered.shape[1] // small - 1
    total = len(pieces)
    slots = products.shape[0] // total
    unlisted = slot_of_ref.shape[1] - 1
    for index, (ref, e) in enumerate(pieces):
        note = ref[e, slots * width :, :].astype(jnp.float32)[0:1, :]
        columns[index : index + 1, :] = note.astype(jnp.int32)
    tell = pltpu.make_async_copy(columns, columns_s, sem)
    tell.start()
    far_ready()
    for index, (ref, e) in enumerate(pieces):
        _, device = source_of(jnp.int32(index))
        for slot in range(slots):
            products[index * slots + slot] = lax.dot_general(
                ref[e, slot * width : (slot + 1) * width, :],
                far_ref[device * slots + slot],
                NT,
                preferred_element_type=jnp.float32,
            )
    tell.wait()
    panel_ready()
    lane_group = lax.broadcasted_iota(jnp.int32, (small, width), 1) // small

    def place_one(index, slot):
        group, device = source_of(index)
        start = group * group_span
        row = where_ref[device * slots + slot]
        idle = row >= fine_rows
        row = jnp.minimum(row, fine_rows - 1)
        wanted, blocks = distinct(
            [columns_s[index, slot * parts + n] + start for n in range(parts)],
            [products[index * slots + slot, n * small : (n + 1) * small, :] for n in range(parts)],
            unlisted,
        )
        for m in range(parts):
            target = pcols_ref[m, row] - base
            owner, within = target // own_rows, lax.rem(target, own_rows)
            shift = lax.rem(within + parts - m, parts) * small
            here = lane_group == within
            places = []
            for column in wanted:
                s = jnp.where(idle, pattern, slot_of_ref[target, column])
                places.append(pl.ds(pl.multiple_of(s * small, small), small))
            sums = [
                gathered[owner, at, :] + jnp.where(here, pltpu.roll(block, shift, 1), 0.0)
                for at, block in zip(places, blocks)
            ]
            for at, value in zip(places, sums):
                gathered[owner, at, :] = value

    def place_source(index, carry):
        for slot in range(slots):
            place_one(index, slot)
        return carry

    lax.fori_loop(0, total, place_source, 0, unroll=16)


def near_kernel(
    first_row, hops, place_ref, acols_ref, pcols_ref, ccols_ref, *refs
):
    resumed = hops > 0
    if resumed:
        where_in, slot_of_ref, pt_ref, a_ref, panel_in, far_in = refs[:6]
        came, refs = refs[6 : 6 + hops], refs[6 + hops :]
        panel_out, far_out, where_ref = refs[:3]
        dense, panel, far, weights, products, sems = refs[3:9]
        landed, far_products, notes, notes_s = refs[9:]
    else:
        ctable_ref, pt_ref, a_ref, panel_out, far_out, where_ref, slot_of_ref = refs[:7]
        dense, panel, far, weights, products, sems = refs[7:]
    step, steps = pl.program_id(0), pl.num_programs(0)
    fine_row = step + first_row
    parts, fine_rows = pcols_ref.shape
    block_cols, width = a_ref.shape[1], pt_ref.shape[1]
    span = width // parts
    pattern = ccols_ref.shape[1]
    slots = far_out.shape[0]
    own_rows = width // span
    base = place_ref[1]
    dump = dense.shape[0] // span - 1
    if resumed:
        load_panel = pltpu.make_async_copy(panel_in, panel, sems.at[0])
        load_far = pltpu.make_async_copy(far_in, far.at[pl.ds(0, slots)], sems.at[1])
        land = [
            pltpu.make_async_copy(one, landed.at[at], sems.at[2 + at]) for at, one in enumerate(came)
        ]

    @pl.when(step == 0)
    def _():
        if resumed:
            for one in [load_panel, load_far] + land:
                one.start()
        else:
            panel[...] = jnp.zeros_like(panel)
            far[...] = jnp.zeros_like(far)
            column = lax.broadcasted_iota(jnp.int32, slot_of_ref.shape, 1)
            found = jnp.full(slot_of_ref.shape, pattern, jnp.int32)
            for s in range(pattern):
                found = jnp.where(column == ctable_ref[:, s : s + 1], s, found)
            slot_of_ref[...] = found

        def begin(slot, carry):
            where_ref[slot] = where_in[slot] if resumed else fine_rows
            return carry

        lax.fori_loop(0, slots, begin, 0)

    dense[...] = jnp.zeros_like(dense)
    left = pt_ref[fine_row]
    for k in range(0, block_cols, 2):
        ahead = range(k, min(k + 2, block_cols))
        weighted = lax.dot_general(
            left,
            jnp.concatenate([a_ref[0, j] for j in ahead], axis=1),
            NN,
            preferred_element_type=jnp.float32,
        ).astype(far.dtype)
        for j in ahead:
            weights[j] = weighted[:, (j - k) * width : (j - k + 1) * width]
    for k in range(block_cols):
        source = acols_ref[fine_row, k]
        row = jnp.where(source >= fine_rows, 0, source)
        products[k] = lax.dot_general(
            pt_ref[row], weights[k], NT, preferred_element_type=jnp.float32
        )
    if resumed:

        @pl.when(step == 0)
        def _():
            load_panel.wait()
            load_far.wait()

    for k in range(block_cols):
        source = acols_ref[fine_row, k]
        is_far = source >= fine_rows
        slot = jnp.where(is_far, source - fine_rows, slots)
        far[slot] = weights[k]
        where_ref[slot] = fine_row
        row = jnp.where(is_far, 0, source)
        columns, blocks = distinct(
            [pcols_ref[n, row] for n in range(parts)],
            [products[k, n * span : (n + 1) * span, :] for n in range(parts)],
            dump,
        )
        places = [
            pl.ds(pl.multiple_of(jnp.where(is_far, dump, column) * span, span), span)
            for column in columns
        ]
        sums = [dense[at, :] + block for at, block in zip(places, blocks)]
        for at, value in zip(places, sums):
            dense[at, :] = value

    lane_group = lax.broadcasted_iota(jnp.int32, (span, width), 1) // span
    for m in range(parts):
        row = pcols_ref[m, fine_row] - base
        owner, within = row // own_rows, lax.rem(row, own_rows)
        shift = lax.rem(within + parts - m, parts) * span
        here = lane_group == within
        for first in range(0, pattern, 9):
            chunk = range(first, min(first + 9, pattern))
            sums = []
            for s in chunk:
                at = pl.ds(pl.multiple_of(ccols_ref[row, s] * span, span), span)
                moved = pltpu.roll(dense[at, :], shift, 1)
                sums.append(
                    panel[owner, s * span : (s + 1) * span, :] + jnp.where(here, moved, 0.0)
                )
            for s, value in zip(chunk, sums):
                panel[owner, s * span : (s + 1) * span, :] = value

    @pl.when(step == steps - 1)
    def _():
        if resumed:
            for one in land:
                one.wait()
            add_slots(
                sources("along", place_ref, 1, 0),
                [(landed.at[at], e) for at in range(hops) for e in range(landed.shape[1])],
                lambda: None, lambda: None, place_ref, where_ref, pcols_ref, slot_of_ref,
                far, panel, far_products, notes, notes_s, sems.at[0],
            )
        one = pltpu.make_async_copy(panel, panel_out, sems.at[0])
        two = pltpu.make_async_copy(far.at[pl.ds(0, slots)], far_out, sems.at[1])
        one.start()
        two.start()
        one.wait()
        two.wait()


def near(first_row, rows_here, place, a_cols, pcols_t, c_cols, pt, a_blocks, owners, all_cols, slots, before=None, came=()):
    rows, cols, span, _ = a_blocks.shape
    parts, width = pcols_t.shape[0], pt.shape[1]
    small = width // parts
    group_rows, pattern = c_cols.shape
    tall = (pattern + 1) * small
    hbm, smem = pl.BlockSpec(memory_space=pltpu.HBM), pl.BlockSpec(memory_space=pltpu.SMEM)
    out_shape = [
        jax.ShapeDtypeStruct((owners, tall, width), jnp.float32),
        jax.ShapeDtypeStruct((slots, width, span), jnp.bfloat16),
        jax.ShapeDtypeStruct((slots + 1,), jnp.int32),
    ]
    out_specs = [hbm, hbm, smem]
    in_specs = [
        whole(rows, width, span),
        pl.BlockSpec((1, cols, span, span), lambda i, *_: (i + first_row, 0, 0, 0)),
    ]
    scalars = [place, a_cols, pcols_t, c_cols]
    if before is None:
        in_specs.insert(0, whole(group_rows, pattern))
        operands = [c_cols, pt, a_blocks]
        out_shape.append(jax.ShapeDtypeStruct((group_rows, all_cols + 128), jnp.int32))
        out_specs.append(whole(group_rows, all_cols + 128))
    else:
        scalars += [before[2], before[3]]
        operands = [pt, a_blocks, before[0], before[1], *came]
        in_specs += [hbm, hbm] + [pl.BlockSpec(memory_space=pl.ANY)] * len(came)
    scratch = [
        (((all_cols + 1) * small, width), jnp.float32),
        ((owners, tall, width), jnp.float32),
        ((slots + 1, width, span), jnp.bfloat16),
        ((cols, width, span), jnp.bfloat16),
        ((cols, width, width), jnp.float32),
    ]
    smem_scratch = []
    if before is not None:
        total = len(came) * came[0].shape[0]
        scratch += [
            ((len(came), *came[0].shape), jnp.bfloat16),
            ((slots // 2, width, width), jnp.float32),
            ((total, span), jnp.int32),
        ]
        smem_scratch = [pltpu.SMEM((total, span), jnp.int32)]
    return pl.pallas_call(
        functools.partial(near_kernel, first_row, len(came)),
        out_shape=tuple(out_shape),
        grid_spec=pltpu.PrefetchScalarGridSpec(
            num_scalar_prefetch=len(scalars),
            grid=(rows_here,),
            in_specs=in_specs,
            out_specs=tuple(out_specs),
            scratch_shapes=[pltpu.VMEM(*one) for one in scratch[:5]]
            + [pltpu.SemaphoreType.DMA((2 + len(came),))]
            + [pltpu.VMEM(*one) for one in scratch[5:]]
            + smem_scratch,
        ),
        compiler_params=pltpu.CompilerParams(
            vmem_limit_bytes=VMEM_MOST
        ),
        cost_estimate=pl.CostEstimate(flops=int(1e11), bytes_accessed=int(1e8), transcendentals=0),
        name="near",
    )(*scalars, *operands)


def far_kernel(
    counts, steps, chips, place_ref, where_in, pcols_ref, slot_of_in, far_in, panel_in, *refs
):
    arrived, refs = refs[: len(counts)], refs[len(counts) :]
    waves = 2 if steps == 1 else 1
    outs, refs = refs[: 2 * waves], refs[2 * waves :]
    panel, far_ref, products, columns, columns_s, sems, *extra = refs
    if steps == 1:
        where_ref, slot_of_ref, *extra = extra
    hidden = bool(extra)
    gathered = extra[0] if hidden else panel
    step = 0 if steps == 1 else pl.program_id(0)
    tall = outs[0].shape[1]
    core, own_chip = place_ref[0], place_ref[2]
    load = pltpu.make_async_copy(panel_in, panel, sems.at[0])
    if steps == 1:
        slots = products.shape[0] // counts[0]
        group_count = counts[0] // chips
        spans = [
            pl.ds(pl.multiple_of((2 * group + 1 - place_ref[3]) * slots * chips, 8), slots * chips)
            for group in range(group_count)
        ]
        loads = [
            pltpu.make_async_copy(far_in.at[one], far_ref.at[one], sems.at[4 + at])
            for at, one in enumerate(spans)
        ]
        loads.append(pltpu.make_async_copy(where_in, where_ref, sems.at[3]))
        loads.append(pltpu.make_async_copy(slot_of_in, slot_of_ref, sems.at[1]))
    else:
        where_ref, slot_of_ref = where_in, slot_of_in
        loads = [pltpu.make_async_copy(far_in, far_ref, sems.at[1])]

    def far_ready():
        for one in loads:
            one.wait()

    def at_start(action):
        action() if steps == 1 else pl.when(step == 0)(action)

    def begin():
        for one in loads:
            one.start()
        load.start()

    at_start(begin)
    if hidden:
        gathered[...] = jnp.zeros_like(gathered)
    add_slots(
        sources("across" if steps == 1 else "both", place_ref, counts[0], step),
        [(arrived[a], e) for a, count in enumerate(counts) for e in range(count)],
        lambda: at_start(far_ready),
        (lambda: None) if hidden else (lambda: at_start(load.wait)),
        place_ref, where_ref, pcols_ref, slot_of_ref, far_ref, gathered,
        products, columns, columns_s, sems.at[2],
    )

    def end():
        if hidden:
            load.wait()

        def take(owner):
            value = panel[owner, 0:tall, :]
            return value + gathered[owner, 0:tall, :] if hidden else value

        for at in range(chips):
            wave, spot = divmod(at, chips // waves)
            send_ref, keep_ref = outs[2 * wave], outs[2 * wave + 1]
            chip = at if waves == 1 else jnp.bitwise_xor(own_chip, chips - 1 - at)
            send_ref[spot] = take(2 * chip + 1 - core).astype(send_ref.dtype)
            keep_ref[spot] = take(2 * chip + core)

    end() if steps == 1 else pl.when(step == steps - 1)(end)


def add_far(place, where, pcols_t, slot_of, arrived, far, panel, chips):
    steps = 8 if len(arrived) == 2 else 1
    waves = 2 if steps == 1 else 1
    payload, span = arrived[0].shape[1:]
    counts = tuple(one.shape[0] // steps for one in arrived)
    width = far.shape[1]
    slot_count = (payload - 16) // width
    owners, padded, _ = panel.shape
    tall = padded - width // pcols_t.shape[0]
    hbm, smem = pl.BlockSpec(memory_space=pltpu.HBM), pl.BlockSpec(memory_space=pltpu.SMEM)
    some = (chips // waves, tall, width)
    outs = ((some, jnp.bfloat16), (some, jnp.float32)) * waves
    held = ((owners, padded, width), jnp.float32)
    scratch = [
        held,
        (far.shape, far.dtype),
        ((sum(counts) * slot_count, width, width), jnp.float32),
        ((sum(counts), span), jnp.int32),
    ]
    scratch_shapes = [pltpu.VMEM(*one) for one in scratch] + [
        pltpu.SMEM((sum(counts), span), jnp.int32),
        pltpu.SemaphoreType.DMA((8,)),
    ]
    if steps == 1:
        scratch_shapes.append(pltpu.SMEM(where.shape, where.dtype))
        scratch_shapes.append(pltpu.SMEM(slot_of.shape, slot_of.dtype))
        vmem = pl.BlockSpec(memory_space=pltpu.VMEM)
        how = dict(
            in_specs=[smem, hbm, smem, hbm, hbm, hbm] + [vmem] * len(arrived),
            out_specs=(vmem,) * len(outs),
            scratch_shapes=scratch_shapes,
        )
    else:
        how = dict(
            grid_spec=pltpu.PrefetchScalarGridSpec(
                num_scalar_prefetch=4,
                grid=(steps,),
                in_specs=[hbm, hbm]
                + [pl.BlockSpec((n, payload, span), lambda i, *_: (i, 0, 0)) for n in counts],
                out_specs=tuple(whole(*shape) for shape, _ in outs),
                scratch_shapes=scratch_shapes,
            )
        )
    return pl.pallas_call(
        functools.partial(far_kernel, counts, steps, chips),
        out_shape=tuple(jax.ShapeDtypeStruct(*one) for one in outs),
        compiler_params=pltpu.CompilerParams(vmem_limit_bytes=FAR_MOST if steps == 1 else VMEM_MOST),
        name="add_far",
        **how,
    )(place, where, pcols_t, slot_of, far, panel, *arrived)


def pair_kernel(keep_ref, got_ref, *out_refs):
    for at, out_ref in enumerate(out_refs):
        out_ref[...] = (keep_ref[at] + got_ref[at].astype(jnp.float32)).astype(out_ref.dtype)


def pair(keep, got, kinds):
    _, tall, width = keep.shape
    vmem = pl.BlockSpec(memory_space=pltpu.VMEM)
    return pl.pallas_call(
        pair_kernel,
        out_shape=tuple(jax.ShapeDtypeStruct((tall, width), kind) for kind in kinds),
        in_specs=[vmem, vmem],
        out_specs=(vmem,) * len(kinds),
        compiler_params=pltpu.CompilerParams(
            vmem_limit_bytes=room(
                (keep.shape, keep.dtype), (got.shape, got.dtype), *[((tall, width), jnp.float32)] * 2
            )
        ),
        name="pair",
    )(keep, got)


def last_kernel(mine_ref, *refs):
    terms, out_ref = refs[:-1], refs[-1]
    total = mine_ref[...]
    for term in terms:
        total = total + term[...].astype(jnp.float32)
    out_ref[...] = total.T.reshape(out_ref.shape)


def last(mine, terms, own_rows):
    tall, width = mine.shape
    vmem = pl.BlockSpec(memory_space=pltpu.VMEM)
    return pl.pallas_call(
        last_kernel,
        out_shape=jax.ShapeDtypeStruct((own_rows, width // own_rows, tall), jnp.float32),
        in_specs=[vmem] * (1 + len(terms)),
        out_specs=vmem,
        compiler_params=pltpu.CompilerParams(vmem_limit_bytes=room(*[(mine.shape, mine.dtype)] * (3 + len(terms)))),
        name="last",
    )(mine, *terms)


def swap(axis, *arrays):
    return [lax.ppermute(one, axis, [(0, 1), (1, 0)]) for one in arrays]


def local(chips, groups, a_blocks, a_cols, p_rows, p_cols, send_rows, c_cols):
    group_rows, parts = c_cols.shape[0], p_cols.shape[1]
    peers, slot_count = send_rows.shape[1:]
    slots = peers * slot_count
    group, half = lax.axis_index("group"), lax.axis_index("zh")
    chip = lax.axis_index(("zh", "zl"))
    low = lax.axis_index("zl")
    place = jnp.stack(
        [lax.axis_index("core"), group * group_rows, chip, half, jnp.int32(chips), group, low]
    ).astype(jnp.int32)
    wanted, pcols_t = send_rows[0].T, p_cols.T
    sizes = (2 * chips, group_rows * groups, slots)
    rows = a_blocks.shape[0]
    facts = jnp.concatenate(
        [wanted, jnp.pad(pcols_t, ((0, 0), (0, peers - pcols_t.shape[1])))], axis=0
    )
    over, facts_over = swap("zh", p_rows, facts)
    scatter = functools.partial(
        lax.all_to_all, axis_name=("group", "zl", "core"), split_axis=0, concat_axis=0, tiled=True
    )
    across = functools.partial(pack, place, slots=slot_count, parts=parts)
    shared = (place, a_cols, pcols_t, c_cols)
    outgoing, pt = across(facts, p_rows, keep_flipped=True)
    came = [scatter(outgoing)]
    if chips == 4:
        before = near(0, FIRST_ROWS, *shared, pt, a_blocks, *sizes)
        over, facts_over, before = lax.optimization_barrier((over, facts_over, before))
        outgoing, = across(facts_over, over, keep_flipped=False)
        outgoing, before = lax.optimization_barrier((outgoing, before))
        arrived = [scatter(outgoing)]
        panel, far, where = near(
            FIRST_ROWS, rows - FIRST_ROWS, *shared, pt, a_blocks, *sizes, before, came
        )
        slot_of = before[3]
    else:
        arrived = came + [scatter(across(facts_over, over, keep_flipped=False)[0])]
        panel, far, where, slot_of = near(0, rows, *shared, pt, a_blocks, *sizes)
    sums = add_far(place, where, pcols_t, slot_of, arrived, far, panel, chips)
    own_rows = group_rows // (2 * chips)
    line = ("zh", "zl")
    if chips == 4:
        give, keep, give_late, keep_late = sums
        got, = swap("core", give)
        out = pair(keep, got, (jnp.bfloat16,) * 2)
        give_late, keep_late, *out = lax.optimization_barrier((give_late, keep_late, *out))
        got_late, = swap("core", give_late)
        out_late, mine = pair(keep_late, got_late, (jnp.bfloat16, jnp.float32))
        terms = [
            lax.ppermute(piece, line, [(q, q ^ off) for q in range(chips)])
            for off, piece in zip((3, 2, 1), [*out, out_late])
        ]
        return last(mine, terms, own_rows)
    give, keep = sums
    got, = swap("core", give)
    both = keep + got.astype(jnp.float32)
    mine = lax.dynamic_index_in_dim(both, chip, 0, keepdims=False)
    came = lax.all_to_all(
        both.astype(jnp.bfloat16), line, split_axis=0, concat_axis=0, tiled=True
    ).astype(jnp.float32)
    other = jnp.arange(chips)[:, None, None] != chip
    return last(mine + jnp.sum(jnp.where(other, came, 0.0), 0), [], own_rows)


def solution(mesh):
    groups, ranks = mesh.shape["group"], mesh.shape["rank"]
    chips = ranks // 2
    every = ("group", "zh", "zl", "core")
    fine = Mesh(mesh.devices.reshape(groups, 2, chips // 2, 2), every)
    in_specs = (P(every), P(every), P(every), P(every), P(every), P("group"))
    return jax.shard_map(
        functools.partial(local, chips, groups),
        mesh=fine,
        in_specs=in_specs,
        out_specs=P(every),
        check_vma=False,
    )
```

```python
import functools
import math

import jax
import jax.numpy as jnp
from jax import lax
from jax.experimental import pallas as pl
from jax.experimental.pallas import tpu as pltpu
from jax.sharding import Mesh, PartitionSpec as P

NT = (((1,), (1,)), ((), ()))
NN = (((1,), (0,)), ((), ()))


VMEM_SLACK = 4 << 20
VMEM_MOST = 56 << 20
PACK_MOST = 60 << 20
FAR_MOST = 50 << 20
FIRST_ROWS = 6


def whole(*shape):
    return pl.BlockSpec(shape, lambda *_: (0,) * len(shape))


def room(*arrays):
    return VMEM_SLACK + sum(math.prod(shape) * jnp.dtype(kind).itemsize for shape, kind in arrays)


def flip(rows_ref, unit, row):
    return lax.dot_general(
        unit, rows_ref[row], NT, preferred_element_type=jnp.float32
    ).astype(rows_ref.dtype)


def identity(width, kind):
    row_id = lax.broadcasted_iota(jnp.int32, (width, width), 0)
    col_id = lax.broadcasted_iota(jnp.int32, (width, width), 1)
    return jnp.where(row_id == col_id, 1.0, 0.0).astype(kind)


def pack_kernel(slots, parts, place_ref, facts_ref, p_in, out_ref, *refs):
    *pt_out, p_ref, pt_ref, sems = refs
    load = pltpu.make_async_copy(p_in, p_ref, sems.at[0])
    load.start()
    load.wait()
    rows, span, width = p_ref.shape
    base, half, low = place_ref[1], place_ref[3], place_ref[4]
    unit = identity(width, p_ref.dtype)
    for row in range(rows):
        pt_ref[row] = flip(p_ref, unit, row)
    saves = [pltpu.make_async_copy(pt_ref, one, sems.at[1]) for one in pt_out]
    for save in saves:
        save.start()
    tail = out_ref.shape[1] - slots * width
    lane = lax.broadcasted_iota(jnp.int32, (tail, span), 1)

    def fill(index, carry):
        device = (2 * (index // low) + half) * low + lax.rem(index, low)
        note = jnp.zeros((tail, span), jnp.int32)
        for slot in range(slots):
            row = jnp.maximum(facts_ref[slot, device], 0)
            out_ref[index, slot * width : (slot + 1) * width, :] = pt_ref[row]
            for part in range(parts):
                column = facts_ref[slots + part, row] - base
                note = jnp.where(lane == slot * parts + part, column, note)
        out_ref[index, slots * width :, :] = note.astype(jnp.float32).astype(out_ref.dtype)
        return carry

    lax.fori_loop(0, out_ref.shape[0], fill, 0)
    for save in saves:
        save.wait()


def pack(place, facts, p_rows, slots, parts, keep_flipped):
    rows, span, width = p_rows.shape
    vmem, smem = pl.BlockSpec(memory_space=pltpu.VMEM), pl.BlockSpec(memory_space=pltpu.SMEM)
    kind = p_rows.dtype
    outgoing = (facts.shape[1] // 2, slots * width + 16, span)
    flipped = (rows, width, span)
    hbm = pl.BlockSpec(memory_space=pltpu.HBM)
    kept = 1 if keep_flipped else 0
    return pl.pallas_call(
        functools.partial(pack_kernel, slots, parts),
        out_shape=(jax.ShapeDtypeStruct(outgoing, kind),)
        + (jax.ShapeDtypeStruct(flipped, kind),) * kept,
        in_specs=[smem, smem, hbm],
        out_specs=(vmem,) + (hbm,) * kept,
        scratch_shapes=[
            pltpu.VMEM(p_rows.shape, kind),
            pltpu.VMEM(flipped, kind),
            pltpu.SemaphoreType.DMA((2,)),
        ],
        compiler_params=pltpu.CompilerParams(
            vmem_limit_bytes=PACK_MOST if kept else room((outgoing, kind), *[(flipped, kind)] * 3)
        ),
        name="pack",
    )(place, facts, p_rows)


def distinct(columns, blocks, dump):
    columns, blocks = list(columns), list(blocks)
    for n in range(1, len(columns)):
        again = jnp.bool_(False)
        for before in range(n):
            same = columns[n] == columns[before]
            blocks[before] = blocks[before] + jnp.where(same, blocks[n], 0.0)
            again = again | same
        columns[n] = jnp.where(again, dump, columns[n])
    return columns, blocks


def sources(kind, place_ref, each, step):
    half, low = place_ref[3], place_ref[4]

    def spread(peer, which):
        group = peer // low
        return group, (2 * group + which) * low + lax.rem(peer, low)

    def along(index):
        return spread(index, half)

    def across(index):
        return spread(index, 1 - half)

    def both(index):
        peer = step * each + lax.rem(index, each)
        return spread(peer, jnp.bitwise_xor(half, index // each))

    return {"along": along, "across": across, "both": both}[kind]


def add_slots(
    source_of, pieces, far_ready, panel_ready, place_ref, where_ref, pcols_ref, slot_of_ref,
    far_ref, gathered, products, columns, columns_s, sem,
):
    parts, fine_rows = pcols_ref.shape
    width = far_ref.shape[1]
    small = width // parts
    own_rows = width // small
    base, group_span = place_ref[1], gathered.shape[0] * own_rows
    pattern = gathered.shape[1] // small - 1
    total = len(pieces)
    slots = products.shape[0] // total
    unlisted = slot_of_ref.shape[1] - 1
    for index, (ref, e) in enumerate(pieces):
        note = ref[e, slots * width :, :].astype(jnp.float32)[0:1, :]
        columns[index : index + 1, :] = note.astype(jnp.int32)
    tell = pltpu.make_async_copy(columns, columns_s, sem)
    tell.start()
    far_ready()
    for index, (ref, e) in enumerate(pieces):
        _, device = source_of(jnp.int32(index))
        for slot in range(slots):
            products[index * slots + slot] = lax.dot_general(
                ref[e, slot * width : (slot + 1) * width, :],
                far_ref[device * slots + slot],
                NT,
                preferred_element_type=jnp.float32,
            )
    tell.wait()
    panel_ready()
    lane_group = lax.broadcasted_iota(jnp.int32, (small, width), 1) // small

    def place_one(index, slot):
        group, device = source_of(index)
        start = group * group_span
        row = where_ref[device * slots + slot]
        idle = row >= fine_rows
        row = jnp.minimum(row, fine_rows - 1)
        wanted, blocks = distinct(
            [columns_s[index, slot * parts + n] + start for n in range(parts)],
            [products[index * slots + slot, n * small : (n + 1) * small, :] for n in range(parts)],
            unlisted,
        )
        for m in range(parts):
            target = pcols_ref[m, row] - base
            owner, within = target // own_rows, lax.rem(target, own_rows)
            shift = lax.rem(within + parts - m, parts) * small
            here = lane_group == within
            places = []
            for column in wanted:
                s = jnp.where(idle, pattern, slot_of_ref[target, column])
                places.append(pl.ds(pl.multiple_of(s * small, small), small))
            sums = [
                gathered[owner, at, :] + jnp.where(here, pltpu.roll(block, shift, 1), 0.0)
                for at, block in zip(places, blocks)
            ]
            for at, value in zip(places, sums):
                gathered[owner, at, :] = value

    def place_source(index, carry):
        for slot in range(slots):
            place_one(index, slot)
        return carry

    lax.fori_loop(0, total, place_source, 0, unroll=16)


def near_kernel(
    first_row, hops, place_ref, acols_ref, pcols_ref, ccols_ref, *refs
):
    resumed = hops > 0
    if resumed:
        where_in, slot_of_ref, pt_ref, a_ref, panel_in, far_in = refs[:6]
        came, refs = refs[6 : 6 + hops], refs[6 + hops :]
        panel_out, far_out, where_ref = refs[:3]
        dense, panel, far, weights, products, sems = refs[3:9]
        landed, far_products, notes, notes_s = refs[9:]
    else:
        ctable_ref, pt_ref, a_ref, panel_out, far_out, where_ref, slot_of_ref = refs[:7]
        dense, panel, far, weights, products, sems = refs[7:]
    step, steps = pl.program_id(0), pl.num_programs(0)
    fine_row = step + first_row
    parts, fine_rows = pcols_ref.shape
    block_cols, width = a_ref.shape[1], pt_ref.shape[1]
    span = width // parts
    pattern = ccols_ref.shape[1]
    slots = far_out.shape[0]
    own_rows = width // span
    base = place_ref[1]
    dump = dense.shape[0] // span - 1
    if resumed:
        load_panel = pltpu.make_async_copy(panel_in, panel, sems.at[0])
        load_far = pltpu.make_async_copy(far_in, far.at[pl.ds(0, slots)], sems.at[1])
        land = [
            pltpu.make_async_copy(one, landed.at[at], sems.at[2 + at]) for at, one in enumerate(came)
        ]

    @pl.when(step == 0)
    def _():
        if resumed:
            for one in [load_panel, load_far] + land:
                one.start()
        else:
            panel[...] = jnp.zeros_like(panel)
            far[...] = jnp.zeros_like(far)
            column = lax.broadcasted_iota(jnp.int32, slot_of_ref.shape, 1)
            found = jnp.full(slot_of_ref.shape, pattern, jnp.int32)
            for s in range(pattern):
                found = jnp.where(column == ctable_ref[:, s : s + 1], s, found)
            slot_of_ref[...] = found

        def begin(slot, carry):
            where_ref[slot] = where_in[slot] if resumed else fine_rows
            return carry

        lax.fori_loop(0, slots, begin, 0)

    dense[...] = jnp.zeros_like(dense)
    left = pt_ref[fine_row]
    for k in range(0, block_cols, 2):
        ahead = range(k, min(k + 2, block_cols))
        weighted = lax.dot_general(
            left,
            jnp.concatenate([a_ref[0, j] for j in ahead], axis=1),
            NN,
            preferred_element_type=jnp.float32,
        ).astype(far.dtype)
        for j in ahead:
            weights[j] = weighted[:, (j - k) * width : (j - k + 1) * width]
    for k in range(block_cols):
        source = acols_ref[fine_row, k]
        row = jnp.where(source >= fine_rows, 0, source)
        products[k] = lax.dot_general(
            pt_ref[row], weights[k], NT, preferred_element_type=jnp.float32
        )
    if resumed:

        @pl.when(step == 0)
        def _():
            load_panel.wait()
            load_far.wait()

    for k in range(block_cols):
        source = acols_ref[fine_row, k]
        is_far = source >= fine_rows
        slot = jnp.where(is_far, source - fine_rows, slots)
        far[slot] = weights[k]
        where_ref[slot] = fine_row
        row = jnp.where(is_far, 0, source)
        columns, blocks = distinct(
            [pcols_ref[n, row] for n in range(parts)],
            [products[k, n * span : (n + 1) * span, :] for n in range(parts)],
            dump,
        )
        places = [
            pl.ds(pl.multiple_of(jnp.where(is_far, dump, column) * span, span), span)
            for column in columns
        ]
        sums = [dense[at, :] + block for at, block in zip(places, blocks)]
        for at, value in zip(places, sums):
            dense[at, :] = value

    lane_group = lax.broadcasted_iota(jnp.int32, (span, width), 1) // span
    for m in range(parts):
        row = pcols_ref[m, fine_row] - base
        owner, within = row // own_rows, lax.rem(row, own_rows)
        shift = lax.rem(within + parts - m, parts) * span
        here = lane_group == within
        for first in range(0, pattern, 9):
            chunk = range(first, min(first + 9, pattern))
            sums = []
            for s in chunk:
                at = pl.ds(pl.multiple_of(ccols_ref[row, s] * span, span), span)
                moved = pltpu.roll(dense[at, :], shift, 1)
                sums.append(
                    panel[owner, s * span : (s + 1) * span, :] + jnp.where(here, moved, 0.0)
                )
            for s, value in zip(chunk, sums):
                panel[owner, s * span : (s + 1) * span, :] = value

    @pl.when(step == steps - 1)
    def _():
        if resumed:
            for one in land:
                one.wait()
            add_slots(
                sources("along", place_ref, 1, 0),
                [(landed.at[at], e) for at in range(hops) for e in range(landed.shape[1])],
                lambda: None, lambda: None, place_ref, where_ref, pcols_ref, slot_of_ref,
                far, panel, far_products, notes, notes_s, sems.at[0],
            )
        one = pltpu.make_async_copy(panel, panel_out, sems.at[0])
        two = pltpu.make_async_copy(far.at[pl.ds(0, slots)], far_out, sems.at[1])
        one.start()
        two.start()
        one.wait()
        two.wait()


def near(first_row, rows_here, place, a_cols, pcols_t, c_cols, pt, a_blocks, owners, all_cols, slots, before=None, came=()):
    rows, cols, span, _ = a_blocks.shape
    parts, width = pcols_t.shape[0], pt.shape[1]
    small = width // parts
    group_rows, pattern = c_cols.shape
    tall = (pattern + 1) * small
    hbm, smem = pl.BlockSpec(memory_space=pltpu.HBM), pl.BlockSpec(memory_space=pltpu.SMEM)
    out_shape = [
        jax.ShapeDtypeStruct((owners, tall, width), jnp.float32),
        jax.ShapeDtypeStruct((slots, width, span), jnp.bfloat16),
        jax.ShapeDtypeStruct((slots + 1,), jnp.int32),
    ]
    out_specs = [hbm, hbm, smem]
    in_specs = [
        whole(rows, width, span),
        pl.BlockSpec((1, cols, span, span), lambda i, *_: (i + first_row, 0, 0, 0)),
    ]
    scalars = [place, a_cols, pcols_t, c_cols]
    if before is None:
        in_specs.insert(0, whole(group_rows, pattern))
        operands = [c_cols, pt, a_blocks]
        out_shape.append(jax.ShapeDtypeStruct((group_rows, all_cols + 128), jnp.int32))
        out_specs.append(whole(group_rows, all_cols + 128))
    else:
        scalars += [before[2], before[3]]
        operands = [pt, a_blocks, before[0], before[1], *came]
        in_specs += [hbm, hbm] + [pl.BlockSpec(memory_space=pl.ANY)] * len(came)
    scratch = [
        (((all_cols + 1) * small, width), jnp.float32),
        ((owners, tall, width), jnp.float32),
        ((slots + 1, width, span), jnp.bfloat16),
        ((cols, width, span), jnp.bfloat16),
        ((cols, width, width), jnp.float32),
    ]
    smem_scratch = []
    if before is not None:
        total = len(came) * came[0].shape[0]
        scratch += [
            ((len(came), *came[0].shape), jnp.bfloat16),
            ((slots // 2, width, width), jnp.float32),
            ((total, span), jnp.int32),
        ]
        smem_scratch = [pltpu.SMEM((total, span), jnp.int32)]
    return pl.pallas_call(
        functools.partial(near_kernel, first_row, len(came)),
        out_shape=tuple(out_shape),
        grid_spec=pltpu.PrefetchScalarGridSpec(
            num_scalar_prefetch=len(scalars),
            grid=(rows_here,),
            in_specs=in_specs,
            out_specs=tuple(out_specs),
            scratch_shapes=[pltpu.VMEM(*one) for one in scratch[:5]]
            + [pltpu.SemaphoreType.DMA((2 + len(came),))]
            + [pltpu.VMEM(*one) for one in scratch[5:]]
            + smem_scratch,
        ),
        compiler_params=pltpu.CompilerParams(
            vmem_limit_bytes=VMEM_MOST
        ),
        cost_estimate=pl.CostEstimate(flops=int(1e11), bytes_accessed=int(1e8), transcendentals=0),
        name="near",
    )(*scalars, *operands)


def far_kernel(
    counts, steps, chips, place_ref, where_in, pcols_ref, slot_of_in, far_in, panel_in, *refs
):
    arrived, refs = refs[: len(counts)], refs[len(counts) :]
    waves = 2 if steps == 1 else 1
    outs, refs = refs[: 2 * waves], refs[2 * waves :]
    panel, far_ref, products, columns, columns_s, sems, *extra = refs
    if steps == 1:
        where_ref, slot_of_ref, *extra = extra
    hidden = bool(extra)
    gathered = extra[0] if hidden else panel
    step = 0 if steps == 1 else pl.program_id(0)
    tall = outs[0].shape[1]
    core, own_chip = place_ref[0], place_ref[2]
    load = pltpu.make_async_copy(panel_in, panel, sems.at[0])
    if steps == 1:
        slots = products.shape[0] // counts[0]
        group_count = counts[0] // chips
        spans = [
            pl.ds(pl.multiple_of((2 * group + 1 - place_ref[3]) * slots * chips, 8), slots * chips)
            for group in range(group_count)
        ]
        loads = [
            pltpu.make_async_copy(far_in.at[one], far_ref.at[one], sems.at[4 + at])
            for at, one in enumerate(spans)
        ]
        loads.append(pltpu.make_async_copy(where_in, where_ref, sems.at[3]))
        loads.append(pltpu.make_async_copy(slot_of_in, slot_of_ref, sems.at[1]))
    else:
        where_ref, slot_of_ref = where_in, slot_of_in
        loads = [pltpu.make_async_copy(far_in, far_ref, sems.at[1])]

    def far_ready():
        for one in loads:
            one.wait()

    def at_start(action):
        action() if steps == 1 else pl.when(step == 0)(action)

    def begin():
        for one in loads:
            one.start()
        load.start()

    at_start(begin)
    if hidden:
        gathered[...] = jnp.zeros_like(gathered)
    add_slots(
        sources("across" if steps == 1 else "both", place_ref, counts[0], step),
        [(arrived[a], e) for a, count in enumerate(counts) for e in range(count)],
        lambda: at_start(far_ready),
        (lambda: None) if hidden else (lambda: at_start(load.wait)),
        place_ref, where_ref, pcols_ref, slot_of_ref, far_ref, gathered,
        products, columns, columns_s, sems.at[2],
    )

    def end():
        if hidden:
            load.wait()

        def take(owner):
            value = panel[owner, 0:tall, :]
            return value + gathered[owner, 0:tall, :] if hidden else value

        for at in range(chips):
            wave, spot = divmod(at, chips // waves)
            send_ref, keep_ref = outs[2 * wave], outs[2 * wave + 1]
            chip = at if waves == 1 else jnp.bitwise_xor(own_chip, chips - 1 - at)
            send_ref[spot] = take(2 * chip + 1 - core).astype(send_ref.dtype)
            keep_ref[spot] = take(2 * chip + core)

    end() if steps == 1 else pl.when(step == steps - 1)(end)


def add_far(place, where, pcols_t, slot_of, arrived, far, panel, chips):
    steps = 8 if len(arrived) == 2 else 1
    waves = 2 if steps == 1 else 1
    payload, span = arrived[0].shape[1:]
    counts = tuple(one.shape[0] // steps for one in arrived)
    width = far.shape[1]
    slot_count = (payload - 16) // width
    owners, padded, _ = panel.shape
    tall = padded - width // pcols_t.shape[0]
    hbm, smem = pl.BlockSpec(memory_space=pltpu.HBM), pl.BlockSpec(memory_space=pltpu.SMEM)
    some = (chips // waves, tall, width)
    outs = ((some, jnp.bfloat16), (some, jnp.float32)) * waves
    held = ((owners, padded, width), jnp.float32)
    scratch = [
        held,
        (far.shape, far.dtype),
        ((sum(counts) * slot_count, width, width), jnp.float32),
        ((sum(counts), span), jnp.int32),
    ]
    scratch_shapes = [pltpu.VMEM(*one) for one in scratch] + [
        pltpu.SMEM((sum(counts), span), jnp.int32),
        pltpu.SemaphoreType.DMA((8,)),
    ]
    if steps == 1:
        scratch_shapes.append(pltpu.SMEM(where.shape, where.dtype))
        scratch_shapes.append(pltpu.SMEM(slot_of.shape, slot_of.dtype))
        vmem = pl.BlockSpec(memory_space=pltpu.VMEM)
        how = dict(
            in_specs=[smem, hbm, smem, hbm, hbm, hbm] + [vmem] * len(arrived),
            out_specs=(vmem,) * len(outs),
            scratch_shapes=scratch_shapes,
        )
    else:
        how = dict(
            grid_spec=pltpu.PrefetchScalarGridSpec(
                num_scalar_prefetch=4,
                grid=(steps,),
                in_specs=[hbm, hbm]
                + [pl.BlockSpec((n, payload, span), lambda i, *_: (i, 0, 0)) for n in counts],
                out_specs=tuple(whole(*shape) for shape, _ in outs),
                scratch_shapes=scratch_shapes,
            )
        )
    if steps == 1:
        where = pltpu.with_memory_space_constraint(where, pltpu.HBM)
    return pl.pallas_call(
        functools.partial(far_kernel, counts, steps, chips),
        out_shape=tuple(jax.ShapeDtypeStruct(*one) for one in outs),
        compiler_params=pltpu.CompilerParams(vmem_limit_bytes=FAR_MOST if steps == 1 else VMEM_MOST),
        name="add_far",
        **how,
    )(place, where, pcols_t, slot_of, far, panel, *arrived)


def pair_kernel(keep_ref, got_ref, *out_refs):
    for at, out_ref in enumerate(out_refs):
        out_ref[...] = (keep_ref[at] + got_ref[at].astype(jnp.float32)).astype(out_ref.dtype)


def pair(keep, got, kinds):
    _, tall, width = keep.shape
    vmem = pl.BlockSpec(memory_space=pltpu.VMEM)
    return pl.pallas_call(
        pair_kernel,
        out_shape=tuple(jax.ShapeDtypeStruct((tall, width), kind) for kind in kinds),
        in_specs=[vmem, vmem],
        out_specs=(vmem,) * len(kinds),
        compiler_params=pltpu.CompilerParams(
            vmem_limit_bytes=room(
                (keep.shape, keep.dtype), (got.shape, got.dtype), *[((tall, width), jnp.float32)] * 2
            )
        ),
        name="pair",
    )(keep, got)


def last_kernel(mine_ref, *refs):
    terms, out_ref = refs[:-1], refs[-1]
    total = mine_ref[...]
    for term in terms:
        total = total + term[...].astype(jnp.float32)
    out_ref[...] = total.T.reshape(out_ref.shape)


def last(mine, terms, own_rows):
    tall, width = mine.shape
    vmem = pl.BlockSpec(memory_space=pltpu.VMEM)
    return pl.pallas_call(
        last_kernel,
        out_shape=jax.ShapeDtypeStruct((own_rows, width // own_rows, tall), jnp.float32),
        in_specs=[vmem] * (1 + len(terms)),
        out_specs=vmem,
        compiler_params=pltpu.CompilerParams(vmem_limit_bytes=room(*[(mine.shape, mine.dtype)] * (3 + len(terms)))),
        name="last",
    )(mine, *terms)


def swap(axis, *arrays):
    return [lax.ppermute(one, axis, [(0, 1), (1, 0)]) for one in arrays]


def local(chips, groups, a_blocks, a_cols, p_rows, p_cols, send_rows, c_cols):
    group_rows, parts = c_cols.shape[0], p_cols.shape[1]
    peers, slot_count = send_rows.shape[1:]
    slots = peers * slot_count
    group, half = lax.axis_index("group"), lax.axis_index("zh")
    chip = lax.axis_index(("zh", "zl"))
    low = lax.axis_index("zl")
    place = jnp.stack(
        [lax.axis_index("core"), group * group_rows, chip, half, jnp.int32(chips), group, low]
    ).astype(jnp.int32)
    wanted, pcols_t = send_rows[0].T, p_cols.T
    sizes = (2 * chips, group_rows * groups, slots)
    rows = a_blocks.shape[0]
    facts = jnp.concatenate(
        [wanted, jnp.pad(pcols_t, ((0, 0), (0, peers - pcols_t.shape[1])))], axis=0
    )
    over, facts_over = swap("zh", p_rows, facts)
    scatter = functools.partial(
        lax.all_to_all, axis_name=("group", "zl", "core"), split_axis=0, concat_axis=0, tiled=True
    )
    across = functools.partial(pack, place, slots=slot_count, parts=parts)
    shared = (place, a_cols, pcols_t, c_cols)
    outgoing, pt = across(facts, p_rows, keep_flipped=True)
    came = [scatter(outgoing)]
    if chips == 4:
        before = near(0, FIRST_ROWS, *shared, pt, a_blocks, *sizes)
        over, facts_over, before = lax.optimization_barrier((over, facts_over, before))
        outgoing, = across(facts_over, over, keep_flipped=False)
        outgoing, before = lax.optimization_barrier((outgoing, before))
        arrived = [scatter(outgoing)]
        panel, far, where = near(
            FIRST_ROWS, rows - FIRST_ROWS, *shared, pt, a_blocks, *sizes, before, came
        )
        slot_of = before[3]
    else:
        arrived = came + [scatter(across(facts_over, over, keep_flipped=False)[0])]
        panel, far, where, slot_of = near(0, rows, *shared, pt, a_blocks, *sizes)
    sums = add_far(place, where, pcols_t, slot_of, arrived, far, panel, chips)
    own_rows = group_rows // (2 * chips)
    line = ("zh", "zl")
    if chips == 4:
        give, keep, give_late, keep_late = sums
        got, = swap("core", give)
        out = pair(keep, got, (jnp.bfloat16,) * 2)
        give_late, keep_late, *out = lax.optimization_barrier((give_late, keep_late, *out))
        got_late, = swap("core", give_late)
        out_late, mine = pair(keep_late, got_late, (jnp.bfloat16, jnp.float32))
        terms = [
            lax.ppermute(piece, line, [(q, q ^ off) for q in range(chips)])
            for off, piece in zip((3, 2, 1), [*out, out_late])
        ]
        return last(mine, terms, own_rows)
    give, keep = sums
    got, = swap("core", give)
    both = keep + got.astype(jnp.float32)
    mine = lax.dynamic_index_in_dim(both, chip, 0, keepdims=False)
    came = lax.all_to_all(
        both.astype(jnp.bfloat16), line, split_axis=0, concat_axis=0, tiled=True
    ).astype(jnp.float32)
    other = jnp.arange(chips)[:, None, None] != chip
    return last(mine + jnp.sum(jnp.where(other, came, 0.0), 0), [], own_rows)


def solution(mesh):
    groups, ranks = mesh.shape["group"], mesh.shape["rank"]
    chips = ranks // 2
    every = ("group", "zh", "zl", "core")
    fine = Mesh(mesh.devices.reshape(groups, 2, chips // 2, 2), every)
    in_specs = (P(every), P(every), P(every), P(every), P(every), P("group"))
    return jax.shard_map(
        functools.partial(local, chips, groups),
        mesh=fine,
        in_specs=in_specs,
        out_specs=P(every),
        check_vma=False,
    )
```
